128 devices in a mesh: gx: 8 (over x, core), gy: 16 (over z, y).
Axes of the slice: x: 4, y: 4, z: 4, core: 2. Of those that a mesh axis runs over, the one named last changes fastest.
Arguments:
- latent: bfloat16 [128, 256, 1024], P('gx', 'gy'), may hold values from -6 to 6
- conv_first: bfloat16 [64, 1728], replicated, may hold values from -0.15625 to 0.15625
- conv_second: bfloat16 [64, 1728], replicated, may hold values from -0.15625 to 0.15625
- w_in: bfloat16 [320, 256], replicated, may hold values from -0.3125 to 0.3125
- w_out: bfloat16 [4, 256], replicated, may hold values from -0.375 to 0.375
- touch: int32 [128, 128], P(('gx', 'gy')), may hold values from -1 to 63, as said below
- anchor: int32 [524288], P(('gx', 'gy')), may hold values from 21 to 8170, as said below
- frac: float32 [3, 524288], P(None, ('gx', 'gy')), may hold values from -0.5 to 0.5
- pfeat: bfloat16 [256, 524288], P(None, ('gx', 'gy')), may hold values from -6 to 6
- cotangent: float32 [4, 524288], P(None, ('gx', 'gy')), may hold values from -48 to 48
Outputs:
- predicted: float32 [4, 524288], P(None, ('gx', 'gy'))
- feature_grads: bfloat16 [256, 524288], P(None, ('gx', 'gy'))
- grid_grad: float32 [128, 256, 1024], P('gx', 'gy')
The draws below stay inside these ranges and needn't reach their ends.
Inputs may be any that keep to these rules, and one draw needn't show every extreme that they name: Row d is device d's touch list: entries o * 1 to o + 1 - 1 name local tiles of owner device o, or -1 for an unused slot; within each such block used slots come first. In every draw some owner is named in all 1 slots of every row, and some other owner in none. For particle p of device d = p // 4096: anchor[p] = s * 4**3 + (ix * 4 + iy) * 4 + iz, where s is a used slot of row d of touch and ix, iy, iz lie in 1 to 2. Every used slot of row d is the slot of some particle of device d.
All inputs are finite; a program needn't handle non-finite values.
Results may differ from the reference program's by a relative error of at most 0.0051.
Values may be sent and summed in bfloat16 or wider, within the bound.
A program may use at most 192 MiB of HBM per device.

```python
import jax
import jax.numpy as jnp
from jax import lax

C = 64
HID = 256
PF = 256
OUT = 4
TS = 4
CAP = 1
CX = 16
CY = 16
NZ = 16
P_DEV = 4096
NX = 128
NY = 256
TILES_DEV = 64
SLOTS = 128
PARTICLES = 524288
N_GX = 8
N_GY = 16
DEVICES = 128


def touch_table(key):
    base = jax.random.fold_in(key, 7)
    key_hot, key_cold, key_count, key_tile, key_pick, key_cell = jax.random.split(base, 6)
    hot_owner = jax.random.randint(key_hot, (), 0, DEVICES)
    cold_owner = (hot_owner + 1 + jax.random.randint(key_cold, (), 0, DEVICES - 1)) % DEVICES
    counts = jax.random.randint(key_count, (DEVICES, DEVICES), 1, CAP + 1)
    owners = jnp.arange(DEVICES, dtype=jnp.int32)[None, :]
    counts = jnp.where(owners == hot_owner, CAP, counts)
    counts = jnp.where(owners == cold_owner, 0, counts)
    tile_ids = jax.random.randint(key_tile, (DEVICES, DEVICES, CAP), 0, TILES_DEV)
    tile_ids = tile_ids.at[0, hot_owner, 0].set(TILES_DEV - 1)
    used = jnp.arange(CAP, dtype=jnp.int32)[None, None, :] < counts[:, :, None]
    touch = jnp.where(used, tile_ids, -1).reshape(DEVICES, DEVICES * CAP).astype(jnp.int32)
    flat_used = used.reshape(DEVICES, DEVICES * CAP).astype(jnp.int32)
    ordering = jnp.argsort(1 - flat_used, axis=1, stable=True).astype(jnp.int32)
    live_slots = jnp.sum(flat_used, axis=1)
    picked = jax.random.randint(key_pick, (DEVICES, P_DEV), 0, live_slots[:, None])
    position = jnp.arange(P_DEV, dtype=jnp.int32)[None, :]
    chosen = jnp.where(position < live_slots[:, None], position, picked)
    slot_of = jnp.take_along_axis(ordering, chosen, axis=1)
    coords = jax.random.randint(key_cell, (3, DEVICES, P_DEV), 1, TS - 1)
    cell_of = (coords[0] * TS + coords[1]) * TS + coords[2]
    anchor = (slot_of * TS ** 3 + cell_of).reshape(DEVICES * P_DEV).astype(jnp.int32)
    return (touch, anchor)


def draw_touch(key, part):
    return touch_table(key)[0]


def draw_anchor(key, part):
    return touch_table(key)[1]


def shard_levels(own_key, shape, shards, smallest, largest):
    gain, own = 1.0, jax.random.fold_in(own_key, 6)
    for dim, blocks in shards:
        heights = jnp.exp(jax.random.uniform(jax.random.fold_in(own, dim), (blocks,), jnp.float32, smallest / len(shards), largest / len(shards)))
        gain = gain * jnp.repeat(heights, shape[dim] // blocks).reshape([-1 if axis == dim else 1 for axis in range(len(shape))])
    return gain


def noise(stream_key, dims, scale, limit, cuts=(), kind=jnp.bfloat16):
    entries = jax.random.normal(stream_key, dims, jnp.float32) * scale
    if len(cuts) > 0:
        entries = shard_levels(stream_key, dims, cuts, -0.22, 0.18) * entries
    return jnp.clip(entries, min=-limit, max=limit).astype(kind)


def setup_inputs(seed: int = 0) -> dict:
    keys = jax.random.split(jax.random.key(seed), 11)
    return {
        "latent": noise(keys[0], (NX, NY, NZ * C), 1.0, 6.0, ((0, 8), (1, 16))),
        "conv_first": noise(keys[1], (C, 27 * C), (27 * C) ** -0.5, 0.15625),
        "conv_second": noise(keys[2], (C, 27 * C), (27 * C) ** -0.5, 0.15625),
        "w_in": noise(keys[3], (C + PF, HID), (C + PF) ** -0.5, 0.3125),
        "w_out": noise(keys[4], (OUT, HID), HID ** -0.5, 0.375),
        "touch": draw_touch(jax.random.fold_in(keys[10], 71), 0),
        "anchor": draw_anchor(jax.random.fold_in(keys[10], 71), 0),
        "frac": jnp.clip(jax.random.uniform(keys[7], (3, PARTICLES), jnp.float32, -0.5, 0.5) * shard_levels(keys[7], (3, PARTICLES), ((1, 128),), -0.4, 0.0), -0.5, 0.5),
        "pfeat": noise(keys[8], (PF, PARTICLES), 1.0, 6.0, ((1, 128),)),
        "cotangent": noise(keys[9], (OUT, PARTICLES), 8.0, 48.0, ((1, 128),), jnp.float32),
    }


def conv_core(padded, weight, rows_x, rows_y, depth_cells, channels):
    cube = padded.reshape(rows_x + 2, rows_y + 2, depth_cells, channels)
    cube = jnp.pad(cube, ((0, 0), (0, 0), (1, 1), (0, 0)))
    pieces = []
    for shift_x in range(3):
        for shift_y in range(3):
            for shift_z in range(3):
                pieces.append(cube[shift_x:shift_x + rows_x, shift_y:shift_y + rows_y, shift_z:shift_z + depth_cells, :])
    stacked = jnp.concatenate(pieces, axis=-1).reshape(-1, 27 * channels)
    summed = lax.dot_general(stacked, weight, (((1,), (1,)), ((), ())), preferred_element_type=jnp.float32)
    return summed.reshape(rows_x, rows_y, depth_cells * channels)

def decode(cell_rows, anchor, frac, features, cotangent, w_in, w_out):
    particle_count = anchor.shape[0]
    block_rows = min(2048, particle_count)
    block_count = particle_count // block_rows
    channels = cell_rows.shape[1]
    neighbor = jnp.arange(27, dtype=jnp.int32)
    step_x = neighbor // 9 - 1
    step_y = neighbor // 3 % 3 - 1
    step_z = neighbor % 3 - 1
    cell_shift = (step_x * (TS * TS) + step_y * TS + step_z).astype(jnp.int32)
    unit_x = step_x.astype(jnp.float32)
    unit_y = step_y.astype(jnp.float32)
    unit_z = step_z.astype(jnp.float32)
    w_sample = w_in[:channels]
    w_state = w_in[channels:]
    w_back = w_out.astype(jnp.float32)

    def advance(block_index, running):
        partial_value, predicted, feature_grads = running
        first_row = block_index * block_rows
        anchor_rows = lax.dynamic_slice_in_dim(anchor, first_row, block_rows, 0)
        offsets = lax.dynamic_slice_in_dim(frac, first_row, block_rows, 1)
        state_rows = lax.dynamic_slice_in_dim(features, first_row, block_rows, 1)
        cot_rows = lax.dynamic_slice_in_dim(cotangent, first_row, block_rows, 1)
        distance = (offsets[0][:, None] - unit_x[None, :]) ** 2 + (offsets[1][:, None] - unit_y[None, :]) ** 2 + (offsets[2][:, None] - unit_z[None, :]) ** 2
        kernel = jnp.exp(-distance)
        weights = kernel / lax.optimization_barrier(jnp.sum(kernel, axis=1, keepdims=True))
        targets = (anchor_rows[:, None] + cell_shift[None, :]).astype(jnp.int32)
        picked = jnp.take(cell_rows, targets, axis=0)
        sampled = lax.optimization_barrier(jnp.sum(weights[:, :, None] * picked.astype(jnp.float32), axis=1)).astype(jnp.bfloat16)
        preact = jnp.dot(sampled, w_sample, preferred_element_type=jnp.float32) + lax.dot_general(state_rows, w_state, (((0,), (0,)), ((), ())), preferred_element_type=jnp.float32)
        active, gelu_back = jax.vjp(jax.nn.gelu, preact)
        active = active.astype(jnp.bfloat16)
        pred_rows = lax.dot_general(w_out, active, (((1,), (1,)), ((), ())), preferred_element_type=jnp.float32)
        grad_active = lax.dot_general(cot_rows, w_back, (((0,), (0,)), ((), ())), precision=lax.Precision.HIGHEST, preferred_element_type=jnp.float32)
        grad_preact = gelu_back(grad_active)[0].astype(jnp.bfloat16)
        grad_state = lax.dot_general(w_state, grad_preact, (((1,), (1,)), ((), ())), preferred_element_type=jnp.float32).astype(jnp.bfloat16)
        grad_sampled = lax.dot_general(grad_preact, w_sample, (((1,), (1,)), ((), ())), preferred_element_type=jnp.float32)
        spread = weights[:, :, None] * grad_sampled[:, None, :]
        partial_value = partial_value.at[targets.reshape(-1)].add(spread.reshape(-1, channels))
        predicted = lax.dynamic_update_slice_in_dim(predicted, pred_rows, first_row, 1)
        feature_grads = lax.dynamic_update_slice_in_dim(feature_grads, grad_state, first_row, 1)
        return (partial_value, predicted, feature_grads)
    initial = (jnp.zeros(cell_rows.shape, jnp.float32), jnp.zeros((w_out.shape[0], particle_count), jnp.float32), jnp.zeros((features.shape[0], particle_count), jnp.bfloat16))
    partial_value, predicted, feature_grads = lax.fori_loop(0, block_count, advance, initial)
    return (predicted, feature_grads, partial_value.astype(jnp.bfloat16))

def reference(latent, conv_first, conv_second, w_in, w_out, touch, anchor, frac, pfeat, cotangent):

    def convolve(field, weight):
        padded = jnp.pad(field, ((1, 1), (1, 1), (0, 0)))
        pieces = [conv_core(padded[slab * CX:slab * CX + CX + 2], weight, CX, NY, NZ, C) for slab in range(N_GX)]
        return jnp.concatenate(pieces, axis=0)
    hidden_field = jax.nn.gelu(convolve(latent, conv_first)).astype(jnp.bfloat16)
    grid_field = (latent.astype(jnp.float32) + convolve(hidden_field, conv_second)).astype(jnp.bfloat16)
    row_width = TS ** 3 * C
    tile_rows = grid_field.reshape(N_GX, CX // TS, TS, N_GY, CY // TS, TS, NZ // TS, TS, C)
    tile_rows = tile_rows.transpose(0, 3, 1, 4, 6, 2, 5, 7, 8).reshape(DEVICES * TILES_DEV, row_width)
    slot_owner = jnp.arange(SLOTS, dtype=jnp.int32) // CAP
    present = touch >= 0
    global_tile = (slot_owner[None, :] * TILES_DEV + jnp.maximum(touch, 0)).astype(jnp.int32)

    def one_device(pieces):
        tile_index, alive, anchor_rows, offsets, state_rows, cot_rows = pieces
        slot_rows = jnp.where(alive[:, None], jnp.take(tile_rows, tile_index, axis=0), jnp.zeros((), jnp.bfloat16))
        return decode(slot_rows.reshape(-1, C), anchor_rows, offsets, state_rows, cot_rows, w_in, w_out)
    frac_dev = frac.reshape(3, DEVICES, P_DEV).transpose(1, 0, 2)
    state_dev = pfeat.reshape(PF, DEVICES, P_DEV).transpose(1, 0, 2)
    cot_dev = cotangent.reshape(OUT, DEVICES, P_DEV).transpose(1, 0, 2)
    predicted, feature_grads, partials = lax.map(one_device, (global_tile, present, anchor.reshape(DEVICES, P_DEV), frac_dev, state_dev, cot_dev))
    predicted = predicted.transpose(1, 0, 2).reshape(OUT, PARTICLES)
    feature_grads = feature_grads.transpose(1, 0, 2).reshape(PF, PARTICLES)
    target = jnp.where(present, global_tile, DEVICES * TILES_DEV).reshape(-1).astype(jnp.int32)
    grad_tiles = jnp.zeros((DEVICES * TILES_DEV, row_width), jnp.float32).at[target].add(partials.reshape(DEVICES * SLOTS, row_width).astype(jnp.float32), mode='drop')
    grid_grad = grad_tiles.reshape(N_GX, N_GY, CX // TS, CY // TS, NZ // TS, TS, TS, TS, C)
    grid_grad = grid_grad.transpose(0, 2, 5, 1, 3, 6, 4, 7, 8).reshape(NX, NY, NZ * C)
    return (predicted, feature_grads, grid_grad)
```

```python
import functools

import jax
import jax.numpy as jnp
from jax import lax
from jax.experimental import pallas as pl
from jax.experimental.pallas import tpu as pltpu
from jax.sharding import PartitionSpec as P

PB = 512

def gelu_pair(x):
    k = 0.7978845608028654
    c = 0.044715
    x2 = x * x
    t = jnp.tanh(k * x * (1.0 + c * x2))
    half = 0.5 * (1.0 + t)
    value = x * half
    slope = half + 0.5 * x * (1.0 - t * t) * (k * (1.0 + 3.0 * c * x2))
    return value, slope

def decode_kernel(x_ref, anchor_ref, frac_ref, feat_ref, cot_ref, w_in_ref, w_out_ref,
                  pred_ref, fg_ref, part_ref, xt_ref, wt_ref, wo_ref, a_ref, acc_ref):
    step = pl.program_id(0)
    slots = x_ref.shape[0] // 16
    pb = anchor_ref.shape[1]

    @pl.when(step == 0)
    def _():
        xt_ref[...] = x_ref[...].T
        wt_ref[...] = w_in_ref[...].T
        wo = w_out_ref[...].astype(jnp.float32).T
        wo_ref[...] = jnp.concatenate([wo, wo, wo, jnp.zeros_like(wo)], axis=1).astype(jnp.bfloat16)
        acc_ref[...] = jnp.zeros_like(acc_ref)

    anchor = anchor_ref[...]
    slot = anchor >> 6
    cell = lax.broadcasted_iota(jnp.int32, (16, pb), 0)
    off_x = (cell >> 2) - ((anchor >> 4) & 3)
    off_y = (cell & 3) - ((anchor >> 2) & 3)
    off_z = lax.broadcasted_iota(jnp.int32, (4, pb), 0) - (anchor & 3)
    dist_x = frac_ref[0:1, :] - off_x.astype(jnp.float32)
    dist_y = frac_ref[1:2, :] - off_y.astype(jnp.float32)
    dist_z = frac_ref[2:3, :] - off_z.astype(jnp.float32)
    near = jnp.logical_and(jnp.abs(off_x) <= 1, jnp.abs(off_y) <= 1)
    kxy = jnp.where(near, jnp.exp(-(dist_x * dist_x + dist_y * dist_y)), 0.0)
    kz = jnp.where(jnp.abs(off_z) <= 1, jnp.exp(-(dist_z * dist_z)), 0.0)
    wxy = (kxy / jnp.sum(kxy, axis=0, keepdims=True)).astype(jnp.bfloat16)
    wz = kz / jnp.sum(kz, axis=0, keepdims=True)

    slot16 = jnp.broadcast_to(slot.astype(jnp.float32), (16, pb)).astype(jnp.bfloat16)
    zero = jnp.zeros_like(wxy)
    for s in range(slots):
        a_ref[s * 16 : (s + 1) * 16, :] = jnp.where(slot16 == jnp.bfloat16(s), wxy, zero)

    mixed = jnp.dot(xt_ref[...], a_ref[...], preferred_element_type=jnp.float32)
    sampled = mixed[0:64] * wz[0:1] + mixed[64:128] * wz[1:2] + mixed[128:192] * wz[2:3] + mixed[192:256] * wz[3:4]
    sampled = sampled.astype(jnp.bfloat16)
    preact = jnp.dot(wt_ref[:, 64:], feat_ref[...], preferred_element_type=jnp.float32) + jnp.dot(
        wt_ref[:, :64], sampled, preferred_element_type=jnp.float32)
    value, slope = gelu_pair(preact)
    pred_ref[...] = jnp.dot(w_out_ref[...], value.astype(jnp.bfloat16), preferred_element_type=jnp.float32)
    cot = cot_ref[...]
    hi = cot.astype(jnp.bfloat16).astype(jnp.float32)
    rest = cot - hi
    mid = rest.astype(jnp.bfloat16).astype(jnp.float32)
    low = rest - mid
    pieces = jnp.concatenate([hi, mid, low, jnp.zeros_like(hi)], axis=0).astype(jnp.bfloat16)
    grad_active = jnp.dot(wo_ref[...], pieces, preferred_element_type=jnp.float32)
    grad_pre = (grad_active * slope).astype(jnp.bfloat16)
    back = jnp.dot(w_in_ref[...], grad_pre, preferred_element_type=jnp.float32)
    fg_ref[...] = back[64:].astype(jnp.bfloat16)
    grad_sampled = back[:64]
    spread = jnp.concatenate([grad_sampled * wz[i : i + 1] for i in range(4)], axis=0).astype(jnp.bfloat16)
    acc_ref[...] += lax.dot_general(a_ref[...], spread, (((1,), (1,)), ((), ())), preferred_element_type=jnp.float32)

    @pl.when(step == pl.num_programs(0) - 1)
    def _():
        part_ref[...] = acc_ref[...].astype(jnp.bfloat16)


def decode(x, anchor, frac, feat, cot, w_in, w_out, interpret=False):
    count = anchor.shape[1]
    rows = x.shape[0]
    whole = lambda a: pl.BlockSpec(a.shape, lambda i: (0, 0))
    col = lambda r: pl.BlockSpec((r, PB), lambda i: (0, i))
    return pl.pallas_call(
        decode_kernel,
        grid=(count // PB,),
        in_specs=[whole(x), col(1), col(3), col(256), col(4), whole(w_in), whole(w_out)],
        out_specs=[col(4), col(256), pl.BlockSpec((rows, 256), lambda i: (0, 0))],
        out_shape=[jax.ShapeDtypeStruct((4, count), jnp.float32), jax.ShapeDtypeStruct((256, count), jnp.bfloat16),
                   jax.ShapeDtypeStruct((rows, 256), jnp.bfloat16)],
        scratch_shapes=[pltpu.VMEM((256, rows), jnp.bfloat16), pltpu.VMEM((256, 320), jnp.bfloat16),
                        pltpu.VMEM((256, 16), jnp.bfloat16), pltpu.VMEM((rows, PB), jnp.bfloat16), pltpu.VMEM((rows, 256), jnp.float32)],
        compiler_params=pltpu.CompilerParams(vmem_limit_bytes=48 << 20),
        interpret=interpret,
        name="decode",
    )(x, anchor, frac, feat, cot, w_in, w_out)


def gelu(x):
    return 0.5 * x * (1.0 + jnp.tanh(0.7978845608028654 * x * (1.0 + 0.044715 * (x * x))))


def pad_z(v):
    gap = jnp.zeros((v.shape[0], 64), v.dtype)
    return jnp.concatenate([gap, v, gap], axis=1)


def spread_weight(w_ref, band_ref):
    for k in range(9):
        tap = w_ref[:, k * 192 : (k + 1) * 192]
        for j in range(4):
            parts = [jnp.zeros((64, j * 64), tap.dtype)] * (j > 0) + [tap] + [jnp.zeros((64, 192 - j * 64), tap.dtype)] * (j < 3)
            band_ref[j * 64 : (j + 1) * 64, k * 384 : (k + 1) * 384] = jnp.concatenate(parts, axis=1)


def shift_rows(stack_ref, index, tile, low, high):
    stack_ref[0, index] = jnp.concatenate([low, tile[:15]], axis=0).astype(jnp.bfloat16)
    stack_ref[1, index] = tile.astype(jnp.bfloat16)
    stack_ref[2, index] = jnp.concatenate([tile[1:], high], axis=0).astype(jnp.bfloat16)


def conv_kernel(pos_ref, table_ref, latent_ref, cols_ref, hx_ref, hy_ref, hc_ref, w1_ref, w2_ref, out_ref,
                band1_ref, band2_ref, rows_ref, edge_ref, hid_ref, hcol_ref, tiles_ref, *, n_gx, n_gy):
    f32 = jnp.float32
    gx, gy = pos_ref[0], pos_ref[1]
    left, right = gx > 0, gx < n_gx - 1
    down, up = gy > 0, gy < n_gy - 1
    x_side, y_side = (left, right), (down, up)
    spread_weight(w1_ref, band1_ref)
    spread_weight(w2_ref, band2_ref)

    def halo_col(side, j):
        mid = hy_ref[side, j].astype(f32)
        low = jnp.where(left, hc_ref[0, side, j].astype(f32), 0.0)
        high = jnp.where(right, hc_ref[1, side, j].astype(f32), 0.0)
        return pad_z(jnp.where(y_side[side], jnp.concatenate([low, mid, high], axis=0), 0.0))

    def own_col(y, c):
        low = [hx_ref[0, i, y : y + 1, :].astype(f32) for i in range(2)]
        high = [hx_ref[1, i, y : y + 1, :].astype(f32) for i in range(2)]
        low = jnp.where(left, jnp.concatenate(low, axis=0), 0.0)
        high = jnp.where(right, jnp.concatenate(high, axis=0), 0.0)
        return pad_z(jnp.concatenate([low, cols_ref[c].astype(f32), high], axis=0))

    lower = [halo_col(0, 0), halo_col(0, 1), own_col(0, 0)]
    upper = [own_col(15, 3), halo_col(1, 0), halo_col(1, 1)]
    fill = jnp.zeros((6, 1152), f32)
    for dx in range(3):
        for dy in range(3):
            edge_ref[dx * 3 + dy] = jnp.concatenate(
                [lower[dy][dx : dx + 18], fill, upper[dy][dx : dx + 18], fill], axis=0).astype(jnp.bfloat16)
    for x in range(20):
        if x < 2:
            tile = jnp.where(left, hx_ref[0, x].astype(f32), 0.0)
        elif x < 18:
            tile = latent_ref[x - 2].astype(f32)
        else:
            tile = jnp.where(right, hx_ref[1, x - 18].astype(f32), 0.0)
        shift_rows(rows_ref, x, pad_z(tile), lower[1][x : x + 1], upper[1][x : x + 1])

    row24 = lax.broadcasted_iota(jnp.int32, (24, 1), 0)
    inside = jnp.logical_and(jnp.logical_or(row24 > 0, left), jnp.logical_or(row24 != 17, right))

    for b in range(4):
        lanes = slice(b * 256, b * 256 + 384)
        taps = []
        for dx in range(3):
            for dy in range(3):
                taps.append(jnp.concatenate([rows_ref[dy, dx : dx + 18, :, lanes].reshape(288, 384), edge_ref[dx * 3 + dy, :, lanes]], axis=0))
        acc = lax.dot_general(jnp.concatenate(taps, axis=1), band1_ref[...], (((1,), (1,)), ((), ())), preferred_element_type=f32)
        acc = gelu(acc)
        out = slice(b * 256, b * 256 + 256)
        hid_ref[0, :, out] = jnp.where(left, acc[:16], 0.0)
        hid_ref[1:17, :, out] = acc[16:272].reshape(16, 16, 256)
        hid_ref[17, :, out] = jnp.where(right, acc[272:288], 0.0)
        hcol_ref[0, :, out] = jnp.where(jnp.logical_and(inside, down), acc[288:312], 0.0)
        hcol_ref[1, :, out] = jnp.where(jnp.logical_and(inside, up), acc[312:336], 0.0)

    low, high = pad_z(hcol_ref[0]), pad_z(hcol_ref[1])
    for x in range(18):
        shift_rows(rows_ref, x, pad_z(hid_ref[x]), low[x : x + 1], high[x : x + 1])

    for b in range(4):
        lanes = slice(b * 256, b * 256 + 384)
        taps = [rows_ref[dy, dx : dx + 16, :, lanes].reshape(256, 384) for dx in range(3) for dy in range(3)]
        acc = lax.dot_general(jnp.concatenate(taps, axis=1), band2_ref[...], (((1,), (1,)), ((), ())), preferred_element_type=f32)
        acc = acc.reshape(16, 16, 256) + latent_ref[:, :, b * 256 : b * 256 + 256].astype(f32)
        for tx in range(4):
            for ty in range(4):
                tile = [acc[tx * 4 + i, ty * 4 : ty * 4 + 4] for i in range(4)]
                tiles_ref[(tx * 4 + ty) * 4 + b] = jnp.concatenate(tile, axis=0).astype(jnp.bfloat16)

    me = gx * n_gy + gy

    def pick(d, carry):
        wanted = table_ref[d, 0, me]
        tile = tiles_ref[jnp.maximum(wanted, 0)]
        out_ref[d] = jnp.where(wanted >= 0, tile, jnp.zeros_like(tile))
        return carry

    lax.fori_loop(0, out_ref.shape[0], pick, 0, unroll=8)


def convolve(pos, table, latent, cols, hx, hy, hc, w1, w2, n_gx, n_gy, interpret=False):
    vm = pl.BlockSpec(memory_space=pltpu.VMEM)
    sm = pl.BlockSpec(memory_space=pltpu.SMEM)
    bf, f32 = jnp.bfloat16, jnp.float32
    return pl.pallas_call(
        functools.partial(conv_kernel, n_gx=n_gx, n_gy=n_gy),
        in_specs=[sm, sm] + [vm] * 7,
        out_specs=vm,
        out_shape=jax.ShapeDtypeStruct((n_gx * n_gy, 16, 256), bf),
        scratch_shapes=[pltpu.VMEM((256, 3456), bf), pltpu.VMEM((256, 3456), bf), pltpu.VMEM((3, 20, 16, 1152), bf),
                        pltpu.VMEM((9, 48, 1152), bf), pltpu.VMEM((18, 16, 1024), f32), pltpu.VMEM((2, 24, 1024), f32),
                        pltpu.VMEM((64, 16, 256), bf)],
        compiler_params=pltpu.CompilerParams(vmem_limit_bytes=48 << 20),
        interpret=interpret,
        name="convolve",
    )(pos, table, latent, cols, hx, hy, hc, w1, w2)


def collect_kernel(pos_ref, table_ref, back_ref, out_ref, sum_ref, *, n_gy):
    me = pos_ref[0] * n_gy + pos_ref[1]
    sum_ref[...] = jnp.zeros_like(sum_ref)

    def add(d, carry):
        wanted = table_ref[d, 0, me]
        row = jnp.where(wanted >= 0, wanted, 64)
        sum_ref[row] += back_ref[d].astype(jnp.float32)
        return carry

    lax.fori_loop(0, back_ref.shape[0], add, 0, unroll=8)
    for tx in range(4):
        for ty in range(4):
            for tz in range(4):
                tile = sum_ref[(tx * 4 + ty) * 4 + tz]
                for i in range(4):
                    out_ref[tx * 4 + i, ty * 4 : ty * 4 + 4, tz * 256 : tz * 256 + 256] = tile[i * 4 : i * 4 + 4]


def collect(pos, table, back, n_gy, interpret=False):
    vm = pl.BlockSpec(memory_space=pltpu.VMEM)
    sm = pl.BlockSpec(memory_space=pltpu.SMEM)
    return pl.pallas_call(
        functools.partial(collect_kernel, n_gy=n_gy),
        in_specs=[sm, sm, vm],
        out_specs=vm,
        out_shape=jax.ShapeDtypeStruct((16, 16, 1024), jnp.float32),
        scratch_shapes=[pltpu.VMEM((65, 16, 256), jnp.float32)],
        compiler_params=pltpu.CompilerParams(vmem_limit_bytes=32 << 20),
        interpret=interpret,
        name="collect",
    )(pos, table, back)


MESH = pl.DeviceIdType.MESH


def peer_of(k, n_gx, n_gy):
    gx, gy = lax.axis_index("gx"), lax.axis_index("gy")
    index = lax.rem(gx * n_gy + gy + k, n_gx * n_gy)
    return index, (index // n_gy, lax.rem(index, n_gy))


def greet_all(n_gx, n_gy):
    barrier = pltpu.get_barrier_semaphore()
    count = n_gx * n_gy

    def signal(k, carry):
        pl.semaphore_signal(barrier, inc=1, device_id=peer_of(k, n_gx, n_gy)[1], device_id_type=MESH)
        return carry

    lax.fori_loop(1, count, signal, 0)
    pl.semaphore_wait(barrier, count - 1)


def trade(source_of, target_ref, own, own_sem, send_sem, recv_sem, n_gx, n_gy):
    count = n_gx * n_gy
    me = lax.axis_index("gx") * n_gy + lax.axis_index("gy")

    def send(k, carry):
        index, device = peer_of(k, n_gx, n_gy)
        pltpu.make_async_remote_copy(src_ref=source_of(index), dst_ref=target_ref.at[me], send_sem=send_sem, recv_sem=recv_sem,
                                     device_id=device, device_id_type=MESH).start()
        return carry

    lax.fori_loop(1, count, send, 0)
    local = pltpu.make_async_copy(own, target_ref.at[me], own_sem)
    local.start()
    return local


def finish(target_ref, local, send_sem, recv_sem, count):
    others = target_ref.at[pl.ds(0, count - 1)]
    local.wait()
    pltpu.make_async_copy(others, others, send_sem).wait()
    pltpu.make_async_copy(others, others, recv_sem).wait()


def swap_kernel(out_ref, in_ref, own_sem, send_sem, recv_sem, *, n_gx, n_gy):
    me = lax.axis_index("gx") * n_gy + lax.axis_index("gy")
    greet_all(n_gx, n_gy)
    local = trade(lambda index: out_ref.at[index], in_ref, out_ref.at[me], own_sem, send_sem, recv_sem, n_gx, n_gy)
    finish(in_ref, local, send_sem, recv_sem, n_gx * n_gy)


def swap(outgoing, n_gx, n_gy, collective_id):
    hbm = pl.BlockSpec(memory_space=pl.ANY)
    dma = pltpu.SemaphoreType.DMA
    return pl.pallas_call(
        functools.partial(swap_kernel, n_gx=n_gx, n_gy=n_gy),
        in_specs=[hbm],
        out_specs=hbm,
        out_shape=jax.ShapeDtypeStruct(outgoing.shape, outgoing.dtype),
        scratch_shapes=[dma(()), dma(()), dma(())],
        compiler_params=pltpu.CompilerParams(collective_id=collective_id, has_side_effects=True),
        name="swap",
    )(outgoing)


def border_kernel(latent_ref, cols_ref, corner_ref, touch_ref, hx_ref, hy_ref, hc_ref, table_ref, pos_ref,
                  own_sem, send_sem, recv_sem, side_send, side_recv, *, n_gx, n_gy):
    gx, gy = lax.axis_index("gx"), lax.axis_index("gy")
    pos_ref[0] = gx
    pos_ref[1] = gy
    greet_all(n_gx, n_gy)
    low_x, high_x = lax.rem(gx + n_gx - 1, n_gx), lax.rem(gx + 1, n_gx)
    low_y, high_y = lax.rem(gy + n_gy - 1, n_gy), lax.rem(gy + 1, n_gy)
    moves = [
        (latent_ref.at[pl.ds(0, 2)], hx_ref.at[1], (low_x, gy)),
        (latent_ref.at[pl.ds(14, 2)], hx_ref.at[0], (high_x, gy)),
        (cols_ref.at[pl.ds(0, 2)], hy_ref.at[1], (gx, low_y)),
        (cols_ref.at[pl.ds(2, 2)], hy_ref.at[0], (gx, high_y)),
    ]
    for i, near_x in enumerate((low_x, high_x)):
        for j, near_y in enumerate((low_y, high_y)):
            moves.append((corner_ref.at[i, j], hc_ref.at[1 - i, 1 - j], (near_x, near_y)))
    copies = []
    for m, (source, target, device) in enumerate(moves):
        copies.append(pltpu.make_async_remote_copy(src_ref=source, dst_ref=target, send_sem=side_send.at[m], recv_sem=side_recv.at[m],
                                                   device_id=device, device_id_type=MESH))
    for copy in copies:
        copy.start()
    local = trade(lambda index: touch_ref.at[0], table_ref, touch_ref.at[0], own_sem, send_sem, recv_sem, n_gx, n_gy)
    for copy in copies:
        copy.wait()
    finish(table_ref, local, send_sem, recv_sem, n_gx * n_gy)


def border(latent, cols, corner, touch, n_gx, n_gy, collective_id):
    hbm = pl.BlockSpec(memory_space=pl.ANY)
    dma = pltpu.SemaphoreType.DMA
    bf = latent.dtype
    width = latent.shape[2]
    shapes = [((2, 2, 16, width), bf), ((2, 2, 16, width), bf), ((2, 2, 2, 2, width), bf),
              ((n_gx * n_gy, 1, n_gx * n_gy), jnp.int32), ((2,), jnp.int32)]
    return pl.pallas_call(
        functools.partial(border_kernel, n_gx=n_gx, n_gy=n_gy),
        in_specs=[hbm] * 4,
        out_specs=[hbm] * 4 + [pl.BlockSpec(memory_space=pltpu.SMEM)],
        out_shape=[jax.ShapeDtypeStruct(s, d) for s, d in shapes],
        scratch_shapes=[dma(()), dma(()), dma(()), dma((8,)), dma((8,))],
        compiler_params=pltpu.CompilerParams(collective_id=collective_id, has_side_effects=True),
        name="border",
    )(latent, cols, corner, touch)


def make_body(n_gx, n_gy):
    def body(latent, conv_first, conv_second, w_in, w_out, touch, anchor, frac, pfeat, cotangent):
        width = latent.shape[2]
        cols = jnp.stack([latent[:, 0], latent[:, 1], latent[:, 14], latent[:, 15]])
        corner = jnp.stack([jnp.stack([cols[2 * j : 2 * j + 2, 14 * i : 14 * i + 2] for j in range(2)]) for i in range(2)])
        hx, hy, hc, table, pos = border(latent, cols, corner, touch.reshape(1, 1, -1), n_gx, n_gy, 0)
        outgoing = convolve(pos, table, latent, cols, hx, hy, hc, conv_first, conv_second, n_gx, n_gy)
        received = swap(outgoing, n_gx, n_gy, 1)
        predicted, feature_grads, partial_sums = decode(
            received.reshape(-1, 256), anchor.reshape(1, -1), frac, pfeat, cotangent, w_in, w_out)
        returned = swap(partial_sums.reshape(received.shape), n_gx, n_gy, 2)
        grid_grad = collect(pos, table, returned, n_gy)
        return (predicted, feature_grads, grid_grad)

    return body


def solution(mesh):
    rows = P(("gx", "gy"), None)
    cols = P(None, ("gx", "gy"))
    grid = P("gx", "gy", None)
    return jax.shard_map(
        make_body(mesh.shape["gx"], mesh.shape["gy"]),
        mesh=mesh,
        in_specs=(grid, P(), P(), P(), P(), rows, P(("gx", "gy")), cols, cols, cols),
        out_specs=(cols, cols, grid),
        check_vma=False,
    )
```

```python
import functools

import jax
import jax.numpy as jnp
from jax import lax
from jax.experimental import pallas as pl
from jax.experimental.pallas import tpu as pltpu
from jax.sharding import PartitionSpec as P


def gelu_pair(x):
    k = 0.7978845608028654
    c = 0.044715
    x2 = x * x
    t = jnp.tanh(k * x * (1.0 + c * x2))
    half = 0.5 * (1.0 + t)
    value = x * half
    slope = half + 0.5 * x * (1.0 - t * t) * (k * (1.0 + 3.0 * c * x2))
    return value, slope


def gelu(x):
    return 0.5 * x * (1.0 + jnp.tanh(0.7978845608028654 * x * (1.0 + 0.044715 * (x * x))))


def pad_z(v):
    gap = jnp.zeros((v.shape[0], 64), v.dtype)
    return jnp.concatenate([gap, v, gap], axis=1)


def spread_weight(w_ref, band_ref):
    for k in range(9):
        tap = w_ref[:, k * 192 : (k + 1) * 192]
        for j in range(4):
            parts = [jnp.zeros((64, j * 64), tap.dtype)] * (j > 0) + [tap] + [jnp.zeros((64, 192 - j * 64), tap.dtype)] * (j < 3)
            band_ref[j * 64 : (j + 1) * 64, k * 384 : (k + 1) * 384] = jnp.concatenate(parts, axis=1)


def shift_rows(stack_ref, index, tile, low, high):
    stack_ref[0, index] = jnp.concatenate([low, tile[:15]], axis=0).astype(jnp.bfloat16)
    stack_ref[1, index] = tile.astype(jnp.bfloat16)
    stack_ref[2, index] = jnp.concatenate([tile[1:], high], axis=0).astype(jnp.bfloat16)


def convolve_block(gx, gy, n_gx, n_gy, latent_ref, cols_ref, hx_ref, hy_ref, hc_ref, band1_ref, band2_ref,
                   rows_ref, edge_ref, hid_ref, hcol_ref, tiles_ref):
    f32 = jnp.float32
    left, right = gx > 0, gx < n_gx - 1
    down, up = gy > 0, gy < n_gy - 1
    x_side, y_side = (left, right), (down, up)

    def halo_col(side, j):
        mid = hy_ref[side, j].astype(f32)
        low = jnp.where(left, hc_ref[0, side, j].astype(f32), 0.0)
        high = jnp.where(right, hc_ref[1, side, j].astype(f32), 0.0)
        return pad_z(jnp.where(y_side[side], jnp.concatenate([low, mid, high], axis=0), 0.0))

    def own_col(y, c):
        low = [hx_ref[0, i, y : y + 1, :].astype(f32) for i in range(2)]
        high = [hx_ref[1, i, y : y + 1, :].astype(f32) for i in range(2)]
        low = jnp.where(left, jnp.concatenate(low, axis=0), 0.0)
        high = jnp.where(right, jnp.concatenate(high, axis=0), 0.0)
        return pad_z(jnp.concatenate([low, cols_ref[c].astype(f32), high], axis=0))

    lower = [halo_col(0, 0), halo_col(0, 1), own_col(0, 0)]
    upper = [own_col(15, 3), halo_col(1, 0), halo_col(1, 1)]
    fill = jnp.zeros((6, 1152), f32)
    for dx in range(3):
        for dy in range(3):
            edge_ref[dx * 3 + dy] = jnp.concatenate(
                [lower[dy][dx : dx + 18], fill, upper[dy][dx : dx + 18], fill], axis=0).astype(jnp.bfloat16)
    for x in range(20):
        if x < 2:
            tile = jnp.where(left, hx_ref[0, x].astype(f32), 0.0)
        elif x < 18:
            tile = latent_ref[x - 2].astype(f32)
        else:
            tile = jnp.where(right, hx_ref[1, x - 18].astype(f32), 0.0)
        shift_rows(rows_ref, x, pad_z(tile), lower[1][x : x + 1], upper[1][x : x + 1])

    row24 = lax.broadcasted_iota(jnp.int32, (24, 1), 0)
    inside = jnp.logical_and(jnp.logical_or(row24 > 0, left), jnp.logical_or(row24 != 17, right))

    for b in range(4):
        lanes = slice(b * 256, b * 256 + 384)
        taps = []
        for dx in range(3):
            for dy in range(3):
                taps.append(jnp.concatenate([rows_ref[dy, dx : dx + 18, :, lanes].reshape(288, 384), edge_ref[dx * 3 + dy, :, lanes]], axis=0))
        acc = lax.dot_general(jnp.concatenate(taps, axis=1), band1_ref[...], (((1,), (1,)), ((), ())), preferred_element_type=f32)
        acc = gelu(acc)
        out = slice(b * 256, b * 256 + 256)
        hid_ref[0, :, out] = jnp.where(left, acc[:16], 0.0)
        hid_ref[1:17, :, out] = acc[16:272].reshape(16, 16, 256)
        hid_ref[17, :, out] = jnp.where(right, acc[272:288], 0.0)
        hcol_ref[0, :, out] = jnp.where(jnp.logical_and(inside, down), acc[288:312], 0.0)
        hcol_ref[1, :, out] = jnp.where(jnp.logical_and(inside, up), acc[312:336], 0.0)

    low, high = pad_z(hcol_ref[0]), pad_z(hcol_ref[1])
    for x in range(18):
        shift_rows(rows_ref, x, pad_z(hid_ref[x]), low[x : x + 1], high[x : x + 1])

    for b in range(4):
        lanes = slice(b * 256, b * 256 + 384)
        taps = [rows_ref[dy, dx : dx + 16, :, lanes].reshape(256, 384) for dx in range(3) for dy in range(3)]
        acc = lax.dot_general(jnp.concatenate(taps, axis=1), band2_ref[...], (((1,), (1,)), ((), ())), preferred_element_type=f32)
        acc = acc.reshape(16, 16, 256) + latent_ref[:, :, b * 256 : b * 256 + 256].astype(f32)
        for tx in range(4):
            for ty in range(4):
                tile = [acc[tx * 4 + i, ty * 4 : ty * 4 + 4] for i in range(4)]
                tiles_ref[(tx * 4 + ty) * 4 + b] = jnp.concatenate(tile, axis=0).astype(jnp.bfloat16)


MESH = pl.DeviceIdType.MESH
PB = 512
CHUNKS = 4


def window_kernel(latent, cols, corner, touch, w1, w2, w_in, w_out, anchor, frac, feat, cot,
                  pred_out, grads_out, back_out, want_out, pos_out,
                  latent_v, cols_v, w1_v, w2_v, w_in_v, w_out_v, anchor_v, frac_v, feat_v, cot_v,
                  hx_v, hy_v, hc_v, table_v, table_s,
                  band1, band2, rows, edge, hid, hcol, tiles, outgoing, received,
                  near, state, lift, mixed, wz_v, wt, wo, active, grad_pre, spread, part, pred_v,
                  load_sem, side_send, side_recv, touch_own, touch_send, touch_recv, smem_sem,
                  tile_send, tile_recv, back_own, back_send, back_recv, store_sem, *, n_gx, n_gy):
    f32, bf16 = jnp.float32, jnp.bfloat16
    count = n_gx * n_gy
    particles = anchor.shape[1]
    blocks = particles // PB
    gx, gy = lax.axis_index("gx"), lax.axis_index("gy")
    me = gx * n_gy + gy
    pos_out[0] = gx
    pos_out[1] = gy

    def device_at(k):
        index = lax.rem(me + k, count)
        return (index // n_gy, lax.rem(index, n_gy))

    loads = [pltpu.make_async_copy(a, b, load_sem.at[i]) for i, (a, b) in enumerate([
        (anchor, anchor_v), (frac, frac_v), (w_in, w_in_v), (w_out, w_out_v), (w1, w1_v), (w2, w2_v),
        (cot, cot_v), (feat, feat_v), (latent, latent_v), (cols, cols_v)])]
    for load in loads:
        load.start()

    barrier = pltpu.get_barrier_semaphore()

    def greet(k, carry):
        pl.semaphore_signal(barrier, inc=1, device_id=device_at(k), device_id_type=MESH)
        return carry

    lax.fori_loop(1, count, greet, 0)

    for load in loads[:6]:
        load.wait()
    wt[...] = w_in_v[...].T
    wide = w_out_v[...].astype(f32).T
    wo[...] = jnp.concatenate([wide, wide, wide, jnp.zeros_like(wide)], axis=1).astype(bf16)
    spread_weight(w1_v, band1)
    spread_weight(w2_v, band2)

    def weigh(i, carry):
        span = pl.ds(pl.multiple_of(i * PB, PB), PB)
        place = anchor_v[:, span]
        offset = frac_v[:, span]
        cell = lax.broadcasted_iota(jnp.int32, (16, PB), 0)
        off_x = (cell >> 2) - ((place >> 4) & 3)
        off_y = (cell & 3) - ((place >> 2) & 3)
        off_z = lax.broadcasted_iota(jnp.int32, (4, PB), 0) - (place & 3)
        dist_x = offset[0:1] - off_x.astype(f32)
        dist_y = offset[1:2] - off_y.astype(f32)
        dist_z = offset[2:3] - off_z.astype(f32)
        beside = jnp.logical_and(jnp.abs(off_x) <= 1, jnp.abs(off_y) <= 1)
        kxy = jnp.where(beside, jnp.exp(-(dist_x * dist_x + dist_y * dist_y)), 0.0)
        kz = jnp.where(jnp.abs(off_z) <= 1, jnp.exp(-(dist_z * dist_z)), 0.0)
        wxy = (kxy / jnp.sum(kxy, axis=0, keepdims=True)).astype(bf16)
        wz_v[:, span] = kz / jnp.sum(kz, axis=0, keepdims=True)
        distance = (me + count - (place >> 6)) & (count - 1)
        distance = jnp.broadcast_to(distance.astype(f32), (16, PB)).astype(bf16)
        zero = jnp.zeros_like(wxy)
        for k in range(count):
            near[k * 16 : (k + 1) * 16, span] = jnp.where(distance == bf16(k), wxy, zero)
        return carry

    lax.fori_loop(0, blocks, weigh, 0)

    pl.semaphore_wait(barrier, count - 1)
    low_x, high_x = lax.rem(gx + n_gx - 1, n_gx), lax.rem(gx + 1, n_gx)
    low_y, high_y = lax.rem(gy + n_gy - 1, n_gy), lax.rem(gy + 1, n_gy)
    moves = [
        (latent.at[pl.ds(0, 2)], hx_v.at[1], (low_x, gy)),
        (latent.at[pl.ds(14, 2)], hx_v.at[0], (high_x, gy)),
        (cols.at[pl.ds(0, 2)], hy_v.at[1], (gx, low_y)),
        (cols.at[pl.ds(2, 2)], hy_v.at[0], (gx, high_y)),
    ]
    for i, near_x in enumerate((low_x, high_x)):
        for j, near_y in enumerate((low_y, high_y)):
            moves.append((corner.at[i, j], hc_v.at[1 - i, 1 - j], (near_x, near_y)))
    sides = [pltpu.make_async_remote_copy(src_ref=a, dst_ref=b, send_sem=side_send.at[m], recv_sem=side_recv.at[m],
                                          device_id=device, device_id_type=MESH) for m, (a, b, device) in enumerate(moves)]
    for copy in sides:
        copy.start()
    own_touch = pltpu.make_async_copy(touch.at[0], table_v.at[me], touch_own)
    own_touch.start()

    def tell(k, carry):
        pltpu.make_async_remote_copy(src_ref=touch.at[0], dst_ref=table_v.at[me], send_sem=touch_send, recv_sem=touch_recv,
                                     device_id=device_at(k), device_id_type=MESH).start()
        return carry

    lax.fori_loop(1, count, tell, 0)

    for load in loads[6:]:
        load.wait()

    def prepare(i, carry):
        span = pl.ds(pl.multiple_of(i * PB, PB), PB)
        state[:, span] = jnp.dot(wt[:, 64:], feat_v[:, span], preferred_element_type=f32)
        given = cot_v[:, span]
        high = given.astype(bf16).astype(f32)
        rest = given - high
        mid = rest.astype(bf16).astype(f32)
        pieces = jnp.concatenate([high, mid, rest - mid, jnp.zeros_like(high)], axis=0).astype(bf16)
        lift[:, span] = jnp.dot(wo[...], pieces, preferred_element_type=f32)
        return carry

    lax.fori_loop(0, blocks, prepare, 0)

    for copy in sides:
        copy.wait()
    convolve_block(gx, gy, n_gx, n_gy, latent_v, cols_v, hx_v, hy_v, hc_v, band1, band2, rows, edge, hid, hcol, tiles)

    own_touch.wait()
    others = table_v.at[pl.ds(0, count - 1)]
    pltpu.make_async_copy(others, others, touch_recv).wait()
    pltpu.make_async_copy(others, others, touch_send).wait()
    to_smem = pltpu.make_async_copy(table_v, table_s, smem_sem)
    to_smem.start()
    to_smem.wait()

    def pick(k, carry):
        wanted = table_s[lax.rem(me + k, count), 0, me]
        want_out[k] = wanted
        tile = tiles[jnp.maximum(wanted, 0)]
        outgoing[k] = jnp.where(wanted >= 0, tile, jnp.zeros_like(tile))
        return carry

    lax.fori_loop(0, count, pick, 0)
    part_slots = count // CHUNKS

    def send_tile(k, carry):
        pltpu.make_async_remote_copy(src_ref=outgoing.at[k], dst_ref=received.at[k], send_sem=tile_send, recv_sem=tile_recv.at[k // part_slots],
                                     device_id=device_at(k), device_id_type=MESH).start()
        return carry

    lax.fori_loop(1, count, send_tile, 0)
    received[0] = outgoing[0]

    for q in range(CHUNKS):
        first = 1 if q == 0 else q * part_slots
        arriving = received.at[pl.ds(first, (q + 1) * part_slots - first)]
        pltpu.make_async_copy(arriving, arriving, tile_recv.at[q]).wait()
        turned = received[q * part_slots : (q + 1) * part_slots].reshape(part_slots * 16, 256).T

        def gather(i, carry):
            span = pl.ds(pl.multiple_of(i * PB, PB), PB)
            value = jnp.dot(turned, near[q * part_slots * 16 : (q + 1) * part_slots * 16, span], preferred_element_type=f32)
            mixed[:, span] = value if q == 0 else mixed[:, span] + value
            return carry

        lax.fori_loop(0, blocks, gather, 0)

    def hidden(i, carry):
        span = pl.ds(pl.multiple_of(i * PB, PB), PB)
        wz = wz_v[:, span]
        sampled = mixed[0:64, span] * wz[0:1]
        for z in range(1, 4):
            sampled = sampled + mixed[z * 64 : z * 64 + 64, span] * wz[z : z + 1]
        preact = state[:, span] + jnp.dot(wt[:, :64], sampled.astype(bf16), preferred_element_type=f32)
        value, slope = gelu_pair(preact)
        active[:, span] = value.astype(bf16)
        grad = (lift[:, span] * slope).astype(bf16)
        grad_pre[:, span] = grad
        back = jnp.dot(w_in_v[0:64, :], grad, preferred_element_type=f32)
        for z in range(4):
            spread[z * 64 : z * 64 + 64, span] = (back * wz[z : z + 1]).astype(bf16)
        return carry

    lax.fori_loop(0, blocks, hidden, 0)

    def scatter(q, carry):
        band = pl.ds(pl.multiple_of(q * part_slots * 16, part_slots * 16), part_slots * 16)
        value = lax.dot_general(near[band, :], spread[...], (((1,), (1,)), ((), ())), preferred_element_type=f32)
        part[pl.ds(q * part_slots, part_slots)] = value.astype(bf16).reshape(part_slots, 16, 256)

        def send_back(j, inner):
            k = q * part_slots + j
            pltpu.make_async_remote_copy(src_ref=part.at[k], dst_ref=back_out.at[k], send_sem=back_send, recv_sem=back_recv,
                                         device_id=device_at(count - k), device_id_type=MESH).start()
            return inner

        return lax.fori_loop(jnp.where(q == 0, 1, 0), part_slots, send_back, carry)

    lax.fori_loop(0, CHUNKS, scatter, 0)
    own_back = pltpu.make_async_copy(part.at[0], back_out.at[0], back_own)
    own_back.start()

    def finish(i, carry):
        span = pl.ds(pl.multiple_of(i * PB, PB), PB)
        pred_v[:, span] = jnp.dot(w_out_v[...], active[:, span], preferred_element_type=f32)
        feat_v[:, span] = jnp.dot(w_in_v[64:, :], grad_pre[:, span], preferred_element_type=f32).astype(bf16)
        return carry

    lax.fori_loop(0, blocks, finish, 0)
    stores = [pltpu.make_async_copy(pred_v, pred_out, store_sem.at[0]), pltpu.make_async_copy(feat_v, grads_out, store_sem.at[1])]
    for store in stores:
        store.start()
    sent = outgoing.at[pl.ds(0, count - 1)]
    pltpu.make_async_copy(sent, sent, tile_send).wait()
    sent = part.at[pl.ds(0, count - 1)]
    pltpu.make_async_copy(sent, sent, back_send).wait()
    own_back.wait()
    for store in stores:
        store.wait()
    landed = back_out.at[pl.ds(0, count - 1)]
    pltpu.make_async_copy(landed, landed, back_recv).wait()


def window(latent, cols, corner, touch, w1, w2, w_in, w_out, anchor, frac, feat, cot, n_gx, n_gy):
    hbm = pl.BlockSpec(memory_space=pl.ANY)
    smem = pl.BlockSpec(memory_space=pltpu.SMEM)
    bf, f32, i32 = jnp.bfloat16, jnp.float32, jnp.int32
    count = n_gx * n_gy
    particles = anchor.shape[1]
    dma = pltpu.SemaphoreType.DMA
    vmem = lambda a: pltpu.VMEM(a.shape, a.dtype)
    shaped = jax.ShapeDtypeStruct
    return pl.pallas_call(
        functools.partial(window_kernel, n_gx=n_gx, n_gy=n_gy),
        in_specs=[hbm] * 12,
        out_specs=[hbm, hbm, hbm, smem, smem],
        out_shape=[shaped((4, particles), f32), shaped((256, particles), bf), shaped((count, 16, 256), bf), shaped((count,), i32), shaped((2,), i32)],
        scratch_shapes=[
            vmem(latent), vmem(cols), vmem(w1), vmem(w2), vmem(w_in), vmem(w_out), vmem(anchor), vmem(frac), vmem(feat), vmem(cot),
            pltpu.VMEM((2, 2, 16, 1024), bf), pltpu.VMEM((2, 2, 16, 1024), bf), pltpu.VMEM((2, 2, 2, 2, 1024), bf),
            pltpu.VMEM((count, 1, count), i32), pltpu.SMEM((count, 1, count), i32),
            pltpu.VMEM((256, 3456), bf), pltpu.VMEM((256, 3456), bf), pltpu.VMEM((3, 20, 16, 1152), bf), pltpu.VMEM((9, 48, 1152), bf),
            pltpu.VMEM((18, 16, 1024), f32), pltpu.VMEM((2, 24, 1024), f32), pltpu.VMEM((64, 16, 256), bf),
            pltpu.VMEM((count, 16, 256), bf), pltpu.VMEM((count, 16, 256), bf),
            pltpu.VMEM((count * 16, particles), bf), pltpu.VMEM((256, particles), f32), pltpu.VMEM((256, particles), f32),
            pltpu.VMEM((256, particles), f32), pltpu.VMEM((4, particles), f32), pltpu.VMEM((256, 320), bf), pltpu.VMEM((256, 16), bf),
            pltpu.VMEM((256, particles), bf), pltpu.VMEM((256, particles), bf), pltpu.VMEM((256, particles), bf),
            pltpu.VMEM((count, 16, 256), bf), pltpu.VMEM((4, particles), f32),
            dma((10,)), dma((8,)), dma((8,)), dma(()), dma(()), dma(()), dma(()),
            dma(()), dma((CHUNKS,)), dma(()), dma(()), dma(()), dma((2,)),
        ],
        compiler_params=pltpu.CompilerParams(collective_id=0, has_side_effects=True, vmem_limit_bytes=62 << 20),
        name="window",
    )(latent, cols, corner, touch, w1, w2, w_in, w_out, anchor, frac, feat, cot)


def collect_kernel(want_ref, back_ref, out_ref, sum_ref):
    sum_ref[...] = jnp.zeros_like(sum_ref)

    def add(k, carry):
        wanted = want_ref[k]
        sum_ref[jnp.where(wanted >= 0, wanted, 64)] += back_ref[k].astype(jnp.float32)
        return carry

    lax.fori_loop(0, back_ref.shape[0], add, 0, unroll=8)
    for tx in range(4):
        for ty in range(4):
            for tz in range(4):
                tile = sum_ref[(tx * 4 + ty) * 4 + tz]
                for i in range(4):
                    out_ref[tx * 4 + i, ty * 4 : ty * 4 + 4, tz * 256 : tz * 256 + 256] = tile[i * 4 : i * 4 + 4]


def collect(want, back):
    return pl.pallas_call(
        collect_kernel,
        in_specs=[pl.BlockSpec(memory_space=pltpu.SMEM), pl.BlockSpec(memory_space=pltpu.VMEM)],
        out_specs=pl.BlockSpec(memory_space=pltpu.VMEM),
        out_shape=jax.ShapeDtypeStruct((16, 16, 1024), jnp.float32),
        scratch_shapes=[pltpu.VMEM((65, 16, 256), jnp.float32)],
        compiler_params=pltpu.CompilerParams(vmem_limit_bytes=32 << 20),
        name="collect",
    )(want, back)


def make_body(n_gx, n_gy):
    def body(latent, conv_first, conv_second, w_in, w_out, touch, anchor, frac, pfeat, cotangent):
        cols = jnp.stack([latent[:, 0], latent[:, 1], latent[:, 14], latent[:, 15]])
        corner = jnp.stack([jnp.stack([cols[2 * j : 2 * j + 2, 14 * i : 14 * i + 2] for j in range(2)]) for i in range(2)])
        predicted, feature_grads, back, want, _ = window(
            latent, cols, corner, touch.reshape(1, 1, -1), conv_first, conv_second, w_in, w_out,
            anchor.reshape(1, -1), frac, pfeat, cotangent, n_gx, n_gy)
        return (predicted, feature_grads, collect(want, back))

    return body


def solution(mesh):
    rows = P(("gx", "gy"), None)
    cols = P(None, ("gx", "gy"))
    grid = P("gx", "gy", None)
    return jax.shard_map(
        make_body(mesh.shape["gx"], mesh.shape["gy"]),
        mesh=mesh,
        in_specs=(grid, P(), P(), P(), P(), rows, P(("gx", "gy")), cols, cols, cols),
        out_specs=(cols, cols, grid),
        check_vma=False,
    )
```

```python
import functools

import jax
import jax.numpy as jnp
from jax import lax
from jax.experimental import pallas as pl
from jax.experimental.pallas import tpu as pltpu
from jax.sharding import PartitionSpec as P


def gelu_pair(x):
    k = 0.7978845608028654
    c = 0.044715
    x2 = x * x
    t = jnp.tanh(k * x * (1.0 + c * x2))
    half = 0.5 * (1.0 + t)
    value = x * half
    slope = half + 0.5 * x * (1.0 - t * t) * (k * (1.0 + 3.0 * c * x2))
    return value, slope


def gelu(x):
    return 0.5 * x * (1.0 + jnp.tanh(0.7978845608028654 * x * (1.0 + 0.044715 * (x * x))))


def pad_z(v):
    gap = jnp.zeros((v.shape[0], 64), v.dtype)
    return jnp.concatenate([gap, v, gap], axis=1)


def spread_weight(w_ref, band_ref):
    for k in range(9):
        tap = w_ref[:, k * 192 : (k + 1) * 192]
        for j in range(4):
            parts = [jnp.zeros((64, j * 64), tap.dtype)] * (j > 0) + [tap] + [jnp.zeros((64, 192 - j * 64), tap.dtype)] * (j < 3)
            band_ref[j * 64 : (j + 1) * 64, k * 384 : (k + 1) * 384] = jnp.concatenate(parts, axis=1)


def shift_rows(stack_ref, index, tile, low, high):
    stack_ref[0, index] = jnp.concatenate([low, tile[:15]], axis=0).astype(jnp.bfloat16)
    stack_ref[1, index] = tile.astype(jnp.bfloat16)
    stack_ref[2, index] = jnp.concatenate([tile[1:], high], axis=0).astype(jnp.bfloat16)


def convolve_first(gx, gy, n_gx, n_gy, latent_ref, cols_ref, hx_ref, hy_ref, hc_ref, band1_ref, rows_ref, edge_ref, hid_ref, hcol_ref):
    f32 = jnp.float32
    left, right = gx > 0, gx < n_gx - 1
    down, up = gy > 0, gy < n_gy - 1
    x_side, y_side = (left, right), (down, up)

    def halo_col(side, j):
        mid = hy_ref[side, j].astype(f32)
        low = jnp.where(left, hc_ref[0, side, j].astype(f32), 0.0)
        high = jnp.where(right, hc_ref[1, side, j].astype(f32), 0.0)
        return pad_z(jnp.where(y_side[side], jnp.concatenate([low, mid, high], axis=0), 0.0))

    def own_col(y, c):
        low = [hx_ref[0, i, y : y + 1, :].astype(f32) for i in range(2)]
        high = [hx_ref[1, i, y : y + 1, :].astype(f32) for i in range(2)]
        low = jnp.where(left, jnp.concatenate(low, axis=0), 0.0)
        high = jnp.where(right, jnp.concatenate(high, axis=0), 0.0)
        return pad_z(jnp.concatenate([low, cols_ref[c].astype(f32), high], axis=0))

    lower = [halo_col(0, 0), halo_col(0, 1), own_col(0, 0)]
    upper = [own_col(15, 3), halo_col(1, 0), halo_col(1, 1)]
    fill = jnp.zeros((6, 1152), f32)
    for dx in range(3):
        for dy in range(3):
            edge_ref[dx * 3 + dy] = jnp.concatenate(
                [lower[dy][dx : dx + 18], fill, upper[dy][dx : dx + 18], fill], axis=0).astype(jnp.bfloat16)
    for x in range(20):
        if x < 2:
            tile = jnp.where(left, hx_ref[0, x].astype(f32), 0.0)
        elif x < 18:
            tile = latent_ref[x - 2].astype(f32)
        else:
            tile = jnp.where(right, hx_ref[1, x - 18].astype(f32), 0.0)
        shift_rows(rows_ref, x, pad_z(tile), lower[1][x : x + 1], upper[1][x : x + 1])

    row24 = lax.broadcasted_iota(jnp.int32, (24, 1), 0)
    inside = jnp.logical_and(jnp.logical_or(row24 > 0, left), jnp.logical_or(row24 != 17, right))

    for b in range(4):
        lanes = slice(b * 256, b * 256 + 384)
        taps = []
        for dx in range(3):
            for dy in range(3):
                taps.append(jnp.concatenate([rows_ref[dy, dx : dx + 18, :, lanes].reshape(288, 384), edge_ref[dx * 3 + dy, :, lanes]], axis=0))
        acc = lax.dot_general(jnp.concatenate(taps, axis=1), band1_ref[...], (((1,), (1,)), ((), ())), preferred_element_type=f32)
        acc = gelu(acc)
        out = slice(b * 256, b * 256 + 256)
        hid_ref[0, :, out] = jnp.where(left, acc[:16], 0.0)
        hid_ref[1:17, :, out] = acc[16:272].reshape(16, 16, 256)
        hid_ref[17, :, out] = jnp.where(right, acc[272:288], 0.0)
        hcol_ref[0, :, out] = jnp.where(jnp.logical_and(inside, down), acc[288:312], 0.0)
        hcol_ref[1, :, out] = jnp.where(jnp.logical_and(inside, up), acc[312:336], 0.0)


def convolve_second(latent_ref, band2_ref, rows_ref, hid_ref, hcol_ref, tiles_ref):
    f32 = jnp.float32
    low, high = pad_z(hcol_ref[0]), pad_z(hcol_ref[1])
    for x in range(18):
        shift_rows(rows_ref, x, pad_z(hid_ref[x]), low[x : x + 1], high[x : x + 1])

    for b in range(4):
        lanes = slice(b * 256, b * 256 + 384)
        taps = [rows_ref[dy, dx : dx + 16, :, lanes].reshape(256, 384) for dx in range(3) for dy in range(3)]
        acc = lax.dot_general(jnp.concatenate(taps, axis=1), band2_ref[...], (((1,), (1,)), ((), ())), preferred_element_type=f32)
        acc = acc.reshape(16, 16, 256) + latent_ref[:, :, b * 256 : b * 256 + 256].astype(f32)
        for tx in range(4):
            for ty in range(4):
                tile = [acc[tx * 4 + i, ty * 4 : ty * 4 + 4] for i in range(4)]
                tiles_ref[(tx * 4 + ty) * 4 + b] = jnp.concatenate(tile, axis=0).astype(jnp.bfloat16)


MESH = pl.DeviceIdType.MESH
PB = 1024
CHUNKS = 8
GROUPS = ((0, 32), (32, 64), (64, 96), (96, 128))


def window_kernel(latent, touch, w1, w2, w_in, w_out, anchor, frac, feat, cot,
                  pred_out, grads_out, back_out, want_out,
                  latent_v, cols_v, corner_v, w1_v, w2_v, w_in_v, w_out_v, anchor_v, frac_v, feat_v, cot_v,
                  hx_v, hy_v, hc_v, table_v, table_s,
                  band1, band2, rows, edge, hid, hcol, tiles, outgoing, received,
                  near, state, lift, mixed, wz_v, wt, wo, active, grad_pre, spread, part, pred_v,
                  load_sem, side_send, side_recv, touch_own, touch_send, touch_recv, smem_sem,
                  tile_send, tile_recv, back_own, back_send, back_recv, store_sem, *, n_gx, n_gy):
    f32, bf16 = jnp.float32, jnp.bfloat16
    count = n_gx * n_gy
    particles = anchor.shape[1]
    blocks = particles // PB
    gx, gy = lax.axis_index("gx"), lax.axis_index("gy")
    me = gx * n_gy + gy

    def device_at(k):
        index = lax.rem(me + k, count)
        return (index // n_gy, lax.rem(index, n_gy))

    loads = [pltpu.make_async_copy(a, b, load_sem.at[i]) for i, (a, b) in enumerate([
        (latent, latent_v), (w1, w1_v), (w2, w2_v), (w_in, w_in_v), (w_out, w_out_v), (cot, cot_v), (feat, feat_v),
        (anchor, anchor_v), (frac, frac_v)])]
    for load in loads:
        load.start()
    own_touch = pltpu.make_async_copy(touch.at[0], table_v.at[me], touch_own)
    own_touch.start()

    along_y = [(gx, lax.rem(gy + j, n_gy)) for j in range(1, n_gy)]
    along_x = [(lax.rem(gx + i, n_gx), gy) for i in range(1, n_gx)]
    low_x, high_x = lax.rem(gx + n_gx - 1, n_gx), lax.rem(gx + 1, n_gx)
    low_y, high_y = lax.rem(gy + n_gy - 1, n_gy), lax.rem(gy + 1, n_gy)
    diagonal = [(near_x, near_y) for near_x in (low_x, high_x) for near_y in (low_y, high_y)]
    barrier = pltpu.get_barrier_semaphore()
    greeted = diagonal + along_x + along_y
    for device in greeted:
        pl.semaphore_signal(barrier, inc=1, device_id=device, device_id_type=MESH)

    loads[0].wait()
    for c, y in enumerate((0, 1, 14, 15)):
        column = jnp.concatenate([latent_v[x, y : y + 1, :].astype(f32) for x in range(16)], axis=0)
        cols_v[c] = column.astype(bf16)
        for i in range(2):
            corner_v[i, c // 2, c % 2] = column[14 * i : 14 * i + 2].astype(bf16)

    pl.semaphore_wait(barrier, len(greeted))
    moves = [
        (latent_v.at[pl.ds(0, 2)], hx_v.at[1], (low_x, gy)),
        (latent_v.at[pl.ds(14, 2)], hx_v.at[0], (high_x, gy)),
        (cols_v.at[pl.ds(0, 2)], hy_v.at[1], (gx, low_y)),
        (cols_v.at[pl.ds(2, 2)], hy_v.at[0], (gx, high_y)),
    ]
    for i, near_x in enumerate((low_x, high_x)):
        for j, near_y in enumerate((low_y, high_y)):
            moves.append((corner_v.at[i, j], hc_v.at[1 - i, 1 - j], (near_x, near_y)))
    sides = [pltpu.make_async_remote_copy(src_ref=a, dst_ref=b, send_sem=side_send.at[m], recv_sem=side_recv.at[m],
                                          device_id=device, device_id_type=MESH) for m, (a, b, device) in enumerate(moves)]
    for copy in sides:
        copy.start()
    for device in along_y:
        pltpu.make_async_remote_copy(src_ref=touch.at[0], dst_ref=table_v.at[me], send_sem=touch_send.at[0], recv_sem=touch_recv.at[0],
                                     device_id=device, device_id_type=MESH).start()

    for load in loads[1:7]:
        load.wait()
    wt[...] = w_in_v[...].T
    wide = w_out_v[...].astype(f32).T
    wo[...] = jnp.concatenate([wide, wide, wide, jnp.zeros_like(wide)], axis=1).astype(bf16)
    spread_weight(w1_v, band1)
    spread_weight(w2_v, band2)

    def prepare(i, carry):
        span = pl.ds(pl.multiple_of(i * PB, PB), PB)
        state[:, span] = jnp.dot(wt[:, 64:], feat_v[:, span], preferred_element_type=f32)
        given = cot_v[:, span]
        high = given.astype(bf16).astype(f32)
        rest = given - high
        mid = rest.astype(bf16).astype(f32)
        pieces = jnp.concatenate([high, mid, rest - mid, jnp.zeros_like(high)], axis=0).astype(bf16)
        lift[:, span] = jnp.dot(wo[...], pieces, preferred_element_type=f32)
        return carry

    lax.fori_loop(0, blocks, prepare, 0)

    for copy in sides:
        copy.wait()
    own_touch.wait()
    line = table_v.at[pl.ds(0, n_gy - 1)]
    pltpu.make_async_copy(line, line, touch_recv.at[0]).wait()
    mine = table_v.at[pl.ds(gx * n_gy, n_gy)]
    for device in along_x:
        pltpu.make_async_remote_copy(src_ref=mine, dst_ref=mine, send_sem=touch_send.at[1], recv_sem=touch_recv.at[1],
                                     device_id=device, device_id_type=MESH).start()
    convolve_first(gx, gy, n_gx, n_gy, latent_v, cols_v, hx_v, hy_v, hc_v, band1, rows, edge, hid, hcol)
    plane = table_v.at[pl.ds(0, count - n_gy)]
    pltpu.make_async_copy(plane, plane, touch_recv.at[1]).wait()
    to_smem = pltpu.make_async_copy(table_v, table_s, smem_sem)
    to_smem.start()
    convolve_second(latent_v, band2, rows, hid, hcol, tiles)
    to_smem.wait()
    pltpu.make_async_copy(line, line, touch_send.at[0]).wait()
    pltpu.make_async_copy(plane, plane, touch_send.at[1]).wait()

    def pick(k, carry):
        wanted = table_s[lax.rem(me + k, count), 0, me]
        want_out[k] = wanted
        tile = tiles[jnp.maximum(wanted, 0)]
        outgoing[k] = jnp.where(wanted >= 0, tile, jnp.zeros_like(tile))
        return carry

    lax.fori_loop(0, count, pick, 0, unroll=8)
    part_slots = count // CHUNKS

    def wait_for(ref, sem):
        pltpu.make_async_copy(ref, ref, sem).wait()

    for g, (first, last) in enumerate(GROUPS):

        def send_tile(k, carry):
            pltpu.make_async_remote_copy(src_ref=outgoing.at[k], dst_ref=received.at[k], send_sem=tile_send, recv_sem=tile_recv.at[g],
                                         device_id=device_at(k), device_id_type=MESH).start()
            return carry

        lax.fori_loop(max(1, first), last, send_tile, 0)
    received[0] = outgoing[0]
    for load in loads[7:]:
        load.wait()

    def weigh(i, carry):
        span = pl.ds(pl.multiple_of(i * PB, PB), PB)
        place = anchor_v[:, span]
        offset = frac_v[:, span]
        cell = lax.broadcasted_iota(jnp.int32, (16, PB), 0)
        off_x = (cell >> 2) - ((place >> 4) & 3)
        off_y = (cell & 3) - ((place >> 2) & 3)
        off_z = lax.broadcasted_iota(jnp.int32, (4, PB), 0) - (place & 3)
        dist_x = offset[0:1] - off_x.astype(f32)
        dist_y = offset[1:2] - off_y.astype(f32)
        dist_z = offset[2:3] - off_z.astype(f32)
        beside = jnp.logical_and(jnp.abs(off_x) <= 1, jnp.abs(off_y) <= 1)
        kxy = jnp.where(beside, jnp.exp(-(dist_x * dist_x + dist_y * dist_y)), 0.0)
        kz = jnp.where(jnp.abs(off_z) <= 1, jnp.exp(-(dist_z * dist_z)), 0.0)
        wxy = (kxy / jnp.sum(kxy, axis=0, keepdims=True)).astype(bf16)
        wz_v[:, span] = kz / jnp.sum(kz, axis=0, keepdims=True)
        distance = (me + count - (place >> 6)) & (count - 1)
        distance = jnp.broadcast_to(distance.astype(f32), (16, PB)).astype(bf16)
        zero = jnp.zeros_like(wxy)
        for k in range(count):
            near[k * 16 : (k + 1) * 16, span] = jnp.where(distance == bf16(k), wxy, zero)
        return carry

    lax.fori_loop(0, blocks, weigh, 0)

    for g, (first, last) in enumerate(GROUPS):
        arrived = max(1, first)
        wait_for(received.at[pl.ds(arrived, last - arrived)], tile_recv.at[g])
        turned = received[first:last].reshape((last - first) * 16, 256).T
        for i in range(blocks):
            span = slice(i * PB, (i + 1) * PB)
            value = jnp.dot(turned, near[first * 16 : last * 16, span], preferred_element_type=f32)
            mixed[:, span] = value if g == 0 else mixed[:, span] + value

    def hidden(i, carry):
        span = pl.ds(pl.multiple_of(i * PB, PB), PB)
        wz = wz_v[:, span]
        sampled = mixed[0:64, span] * wz[0:1]
        for z in range(1, 4):
            sampled = sampled + mixed[z * 64 : z * 64 + 64, span] * wz[z : z + 1]
        preact = state[:, span] + jnp.dot(wt[:, :64], sampled.astype(bf16), preferred_element_type=f32)
        value, slope = gelu_pair(preact)
        active[:, span] = value.astype(bf16)
        grad = (lift[:, span] * slope).astype(bf16)
        grad_pre[:, span] = grad
        back = jnp.dot(w_in_v[0:64, :], grad, preferred_element_type=f32)
        for z in range(4):
            spread[z * 64 : z * 64 + 64, span] = (back * wz[z : z + 1]).astype(bf16)
        return carry

    lax.fori_loop(0, blocks, hidden, 0)

    def scatter(q, carry):
        band = pl.ds(pl.multiple_of(q * part_slots * 16, part_slots * 16), part_slots * 16)
        value = lax.dot_general(near[band, :], spread[...], (((1,), (1,)), ((), ())), preferred_element_type=f32)
        part[pl.ds(q * part_slots, part_slots)] = value.astype(bf16).reshape(part_slots, 16, 256)

        def send_back(j, inner):
            k = q * part_slots + j
            pltpu.make_async_remote_copy(src_ref=part.at[k], dst_ref=back_out.at[k], send_sem=back_send, recv_sem=back_recv,
                                         device_id=device_at(count - k), device_id_type=MESH).start()
            return inner

        return lax.fori_loop(jnp.where(q == 0, 1, 0), part_slots, send_back, carry)

    lax.fori_loop(0, CHUNKS, scatter, 0)
    own_back = pltpu.make_async_copy(part.at[0], back_out.at[0], back_own)
    own_back.start()

    def finish(i, carry):
        span = pl.ds(pl.multiple_of(i * PB, PB), PB)
        pred_v[:, span] = jnp.dot(w_out_v[...], active[:, span], preferred_element_type=f32)
        feat_v[:, span] = jnp.dot(w_in_v[64:, :], grad_pre[:, span], preferred_element_type=f32).astype(bf16)
        return carry

    lax.fori_loop(0, blocks, finish, 0)
    stores = [pltpu.make_async_copy(pred_v, pred_out, store_sem.at[0]), pltpu.make_async_copy(feat_v, grads_out, store_sem.at[1])]
    for store in stores:
        store.start()
    wait_for(outgoing.at[pl.ds(0, count - 1)], tile_send)
    sent = part.at[pl.ds(0, count - 1)]
    pltpu.make_async_copy(sent, sent, back_send).wait()
    own_back.wait()
    for store in stores:
        store.wait()
    landed = back_out.at[pl.ds(0, count - 1)]
    pltpu.make_async_copy(landed, landed, back_recv).wait()


def window(latent, touch, w1, w2, w_in, w_out, anchor, frac, feat, cot, n_gx, n_gy):
    hbm = pl.BlockSpec(memory_space=pltpu.HBM)
    smem = pl.BlockSpec(memory_space=pltpu.SMEM)
    bf, f32, i32 = jnp.bfloat16, jnp.float32, jnp.int32
    count = n_gx * n_gy
    particles = anchor.shape[1]
    dma = pltpu.SemaphoreType.DMA
    vmem = lambda a: pltpu.VMEM(a.shape, a.dtype)
    shaped = jax.ShapeDtypeStruct
    return pl.pallas_call(
        functools.partial(window_kernel, n_gx=n_gx, n_gy=n_gy),
        in_specs=[hbm] * 10,
        out_specs=[hbm, hbm, hbm, smem],
        out_shape=[shaped((4, particles), f32), shaped((256, particles), bf), shaped((count, 16, 256), bf), shaped((count,), i32)],
        scratch_shapes=[
            vmem(latent), pltpu.VMEM((4, 16, 1024), bf), pltpu.VMEM((2, 2, 2, 2, 1024), bf), vmem(w1), vmem(w2), vmem(w_in), vmem(w_out), vmem(anchor), vmem(frac), vmem(feat), vmem(cot),
            pltpu.VMEM((2, 2, 16, 1024), bf), pltpu.VMEM((2, 2, 16, 1024), bf), pltpu.VMEM((2, 2, 2, 2, 1024), bf),
            pltpu.VMEM((count, 1, count), i32), pltpu.SMEM((count, 1, count), i32),
            pltpu.VMEM((256, 3456), bf), pltpu.VMEM((256, 3456), bf), pltpu.VMEM((3, 20, 16, 1152), bf), pltpu.VMEM((9, 48, 1152), bf),
            pltpu.VMEM((18, 16, 1024), f32), pltpu.VMEM((2, 24, 1024), f32), pltpu.VMEM((64, 16, 256), bf),
            pltpu.VMEM((count, 16, 256), bf), pltpu.VMEM((count, 16, 256), bf),
            pltpu.VMEM((count * 16, particles), bf), pltpu.VMEM((256, particles), f32), pltpu.VMEM((256, particles), f32),
            pltpu.VMEM((256, particles), f32), pltpu.VMEM((4, particles), f32), pltpu.VMEM((256, 320), bf), pltpu.VMEM((256, 16), bf),
            pltpu.VMEM((256, particles), bf), pltpu.VMEM((256, particles), bf), pltpu.VMEM((256, particles), bf),
            pltpu.VMEM((count, 16, 256), bf), pltpu.VMEM((4, particles), f32),
            dma((9,)), dma((8,)), dma((8,)), dma(()), dma((2,)), dma((2,)), dma(()),
            dma(()), dma((len(GROUPS),)), dma(()), dma(()), dma(()), dma((2,)),
        ],
        compiler_params=pltpu.CompilerParams(collective_id=0, has_side_effects=True, vmem_limit_bytes=62 << 20),
        name="window",
    )(latent, touch, w1, w2, w_in, w_out, anchor, frac, feat, cot)


LANES = 4


def collect_kernel(want_ref, back, pred_in, grads_in, grid_out, pred_out, grads_out, back_v, pred_v, grads_v, grid_v, *rest):
    sums, load_sem, store_sem = rest[:LANES], rest[LANES], rest[LANES + 1]
    loads = [pltpu.make_async_copy(a, b, load_sem.at[i]) for i, (a, b) in enumerate([(back, back_v), (grads_in, grads_v), (pred_in, pred_v)])]
    for load in loads:
        load.start()
    for sum_ref in sums:
        sum_ref[...] = jnp.zeros_like(sum_ref)
    loads[0].wait()

    def add(j, carry):
        for lane, sum_ref in enumerate(sums):
            k = j * LANES + lane
            wanted = want_ref[k]
            sum_ref[jnp.where(wanted >= 0, wanted, 64)] += back_v[k].astype(jnp.float32)
        return carry

    lax.fori_loop(0, back_v.shape[0] // LANES, add, 0, unroll=4)
    loads[1].wait()
    loads[2].wait()
    stores = [pltpu.make_async_copy(a, b, store_sem.at[i]) for i, (a, b) in enumerate([(grads_v, grads_out), (pred_v, pred_out), (grid_v, grid_out)])]
    stores[0].start()
    stores[1].start()
    for tx in range(4):
        for ty in range(4):
            for tz in range(4):
                t = (tx * 4 + ty) * 4 + tz
                tile = sums[0][t]
                for sum_ref in sums[1:]:
                    tile = tile + sum_ref[t]
                for i in range(4):
                    grid_v[tx * 4 + i, ty * 4 : ty * 4 + 4, tz * 256 : tz * 256 + 256] = tile[i * 4 : i * 4 + 4]
    stores[2].start()
    for store in stores:
        store.wait()


def collect(want, back, predicted, grads):
    hbm = pl.BlockSpec(memory_space=pltpu.HBM)
    shaped = jax.ShapeDtypeStruct
    vmem = lambda a: pltpu.VMEM(a.shape, a.dtype)
    grid = shaped((16, 16, 1024), jnp.float32)
    return pl.pallas_call(
        collect_kernel,
        in_specs=[pl.BlockSpec(memory_space=pltpu.SMEM), hbm, hbm, hbm],
        out_specs=[hbm, hbm, hbm],
        out_shape=[grid, shaped(predicted.shape, predicted.dtype), shaped(grads.shape, grads.dtype)],
        scratch_shapes=[vmem(back), vmem(predicted), vmem(grads), vmem(grid)] + [pltpu.VMEM((65, 16, 256), jnp.float32)] * LANES
        + [pltpu.SemaphoreType.DMA((3,)), pltpu.SemaphoreType.DMA((3,))],
        compiler_params=pltpu.CompilerParams(vmem_limit_bytes=62 << 20),
        name="collect",
    )(want, back, predicted, grads)


def make_body(n_gx, n_gy):
    def body(latent, conv_first, conv_second, w_in, w_out, touch, anchor, frac, pfeat, cotangent):
        predicted, grads, back, want = window(
            latent, touch.reshape(1, 1, -1), conv_first, conv_second, w_in, w_out, anchor.reshape(1, -1), frac, pfeat, cotangent, n_gx, n_gy)
        grid_grad, predicted, grads = collect(want, back, predicted, grads)
        return (predicted, grads, grid_grad)

    return body


def solution(mesh):
    rows = P(("gx", "gy"), None)
    cols = P(None, ("gx", "gy"))
    grid = P("gx", "gy", None)
    return jax.shard_map(
        make_body(mesh.shape["gx"], mesh.shape["gy"]),
        mesh=mesh,
        in_specs=(grid, P(), P(), P(), P(), rows, P(("gx", "gy")), cols, cols, cols),
        out_specs=(cols, cols, grid),
        check_vma=False,
    )
```

```python
import functools

import jax
import jax.numpy as jnp
from jax import lax
from jax.experimental import pallas as pl
from jax.experimental.pallas import tpu as pltpu
from jax.sharding import PartitionSpec as P


def gelu_pair(x):
    k = 0.7978845608028654
    c = 0.044715 * k
    x2 = x * x
    share = 0.5 * jnp.tanh(x * (k + c * x2)) + 0.5
    slope = share * (1.0 + (1.0 - share) * (x * (2.0 * k + 6.0 * c * x2)))
    return x * share, slope


def gelu(x):
    return 0.5 * x * (1.0 + jnp.tanh(0.7978845608028654 * x * (1.0 + 0.044715 * (x * x))))


def pad_z(v):
    gap = jnp.zeros((v.shape[0], 64), v.dtype)
    return jnp.concatenate([gap, v, gap], axis=1)


def spread_weight(w_ref, band_ref):
    for k in range(9):
        tap = w_ref[:, k * 192 : (k + 1) * 192]
        for j in range(4):
            parts = [jnp.zeros((64, j * 64), tap.dtype)] * (j > 0) + [tap] + [jnp.zeros((64, 192 - j * 64), tap.dtype)] * (j < 3)
            band_ref[j * 64 : (j + 1) * 64, k * 384 : (k + 1) * 384] = jnp.concatenate(parts, axis=1)


def shift_rows(stack_ref, index, tile, low, high):
    stack_ref[0, index] = jnp.concatenate([low, tile[:15]], axis=0).astype(jnp.bfloat16)
    stack_ref[1, index] = tile.astype(jnp.bfloat16)
    stack_ref[2, index] = jnp.concatenate([tile[1:], high], axis=0).astype(jnp.bfloat16)


def convolve_first(gx, gy, n_gx, n_gy, latent_ref, cols_ref, hx_ref, hy_ref, hc_ref, band1_ref, rows_ref, edge_ref, hid_ref, hcol_ref):
    f32 = jnp.float32
    left, right = gx > 0, gx < n_gx - 1
    down, up = gy > 0, gy < n_gy - 1
    x_side, y_side = (left, right), (down, up)

    def halo_col(side, j):
        mid = hy_ref[side, j].astype(f32)
        low = jnp.where(left, hc_ref[0, side, j].astype(f32), 0.0)
        high = jnp.where(right, hc_ref[1, side, j].astype(f32), 0.0)
        return pad_z(jnp.where(y_side[side], jnp.concatenate([low, mid, high], axis=0), 0.0))

    def own_col(y, c):
        low = [hx_ref[0, i, y : y + 1, :].astype(f32) for i in range(2)]
        high = [hx_ref[1, i, y : y + 1, :].astype(f32) for i in range(2)]
        low = jnp.where(left, jnp.concatenate(low, axis=0), 0.0)
        high = jnp.where(right, jnp.concatenate(high, axis=0), 0.0)
        return pad_z(jnp.concatenate([low, cols_ref[c].astype(f32), high], axis=0))

    lower = [halo_col(0, 0), halo_col(0, 1), own_col(0, 0)]
    upper = [own_col(15, 3), halo_col(1, 0), halo_col(1, 1)]
    fill = jnp.zeros((6, 1152), f32)
    for dx in range(3):
        for dy in range(3):
            edge_ref[dx * 3 + dy] = jnp.concatenate(
                [lower[dy][dx : dx + 18], fill, upper[dy][dx : dx + 18], fill], axis=0).astype(jnp.bfloat16)
    for x in range(20):
        if x < 2:
            tile = jnp.where(left, hx_ref[0, x].astype(f32), 0.0)
        elif x < 18:
            tile = latent_ref[x - 2].astype(f32)
        else:
            tile = jnp.where(right, hx_ref[1, x - 18].astype(f32), 0.0)
        shift_rows(rows_ref, x, pad_z(tile), lower[1][x : x + 1], upper[1][x : x + 1])

    row24 = lax.broadcasted_iota(jnp.int32, (24, 1), 0)
    inside = jnp.logical_and(jnp.logical_or(row24 > 0, left), jnp.logical_or(row24 != 17, right))

    for b in range(4):
        lanes = slice(b * 256, b * 256 + 384)
        taps = []
        for dx in range(3):
            for dy in range(3):
                taps.append(jnp.concatenate([rows_ref[dy, dx : dx + 18, :, lanes].reshape(288, 384), edge_ref[dx * 3 + dy, :, lanes]], axis=0))
        acc = lax.dot_general(jnp.concatenate(taps, axis=1), band1_ref[...], (((1,), (1,)), ((), ())), preferred_element_type=f32)
        acc = gelu(acc)
        out = slice(b * 256, b * 256 + 256)
        hid_ref[0, :, out] = jnp.where(left, acc[:16], 0.0)
        hid_ref[1:17, :, out] = acc[16:272].reshape(16, 16, 256)
        hid_ref[17, :, out] = jnp.where(right, acc[272:288], 0.0)
        hcol_ref[0, :, out] = jnp.where(jnp.logical_and(inside, down), acc[288:312], 0.0)
        hcol_ref[1, :, out] = jnp.where(jnp.logical_and(inside, up), acc[312:336], 0.0)


def convolve_second(latent_ref, band2_ref, rows_ref, hid_ref, hcol_ref, tiles_ref):
    f32 = jnp.float32
    low, high = pad_z(hcol_ref[0]), pad_z(hcol_ref[1])
    for x in range(18):
        shift_rows(rows_ref, x, pad_z(hid_ref[x]), low[x : x + 1], high[x : x + 1])

    for b in range(4):
        lanes = slice(b * 256, b * 256 + 384)
        taps = [rows_ref[dy, dx : dx + 16, :, lanes].reshape(256, 384) for dx in range(3) for dy in range(3)]
        acc = lax.dot_general(jnp.concatenate(taps, axis=1), band2_ref[...], (((1,), (1,)), ((), ())), preferred_element_type=f32)
        acc = acc.reshape(16, 16, 256) + latent_ref[:, :, b * 256 : b * 256 + 256].astype(f32)
        for tx in range(4):
            for ty in range(4):
                tile = [acc[tx * 4 + i, ty * 4 : ty * 4 + 4] for i in range(4)]
                tiles_ref[(tx * 4 + ty) * 4 + b] = jnp.concatenate(tile, axis=0).astype(jnp.bfloat16)


MESH = pl.DeviceIdType.MESH
PB = 1024
CHUNKS = 4
SPAN = 1024
STRIP = 16
GROUPS = ((0, 32), (32, 64), (64, 96), (96, 128))


def window_kernel(latent, touch, w1, w2, w_in, w_out, anchor, frac, feat, cot,
                  pred_out, grads_out, back_out, want_out,
                  latent_v, cols_v, corner_v, w1_v, w2_v, w_in_v, w_out_v, anchor_v, frac_v, feat_v, cot_v,
                  hx_v, hy_v, hc_v, table_v, table_s,
                  band1, band2, rows, edge, hid, hcol, tiles, outgoing, received,
                  near, state, lift, mixed, wz_v, wt, wo, active, grad_pre, spread, part, pred_v,
                  load_sem, side_send, side_recv, touch_own, touch_send, touch_recv, smem_sem,
                  tile_send, tile_recv, back_own, back_send, back_recv, store_sem, *, n_gx, n_gy):
    f32, bf16 = jnp.float32, jnp.bfloat16
    count = n_gx * n_gy
    particles = anchor.shape[1]
    blocks = particles // PB
    gx, gy = lax.axis_index("gx"), lax.axis_index("gy")
    me = gx * n_gy + gy

    def device_at(k):
        index = lax.rem(me + k, count)
        return (index // n_gy, lax.rem(index, n_gy))

    along_y = [(gx, lax.rem(gy + j, n_gy)) for j in range(1, n_gy)]
    along_x = [(lax.rem(gx + i, n_gx), gy) for i in range(1, n_gx)]
    low_x, high_x = lax.rem(gx + n_gx - 1, n_gx), lax.rem(gx + 1, n_gx)
    low_y, high_y = lax.rem(gy + n_gy - 1, n_gy), lax.rem(gy + 1, n_gy)
    diagonal = [(near_x, near_y) for near_x in (low_x, high_x) for near_y in (low_y, high_y)]
    barrier = pltpu.get_barrier_semaphore()
    greeted = diagonal + along_x + along_y
    for device in greeted:
        pl.semaphore_signal(barrier, inc=1, device_id=device, device_id_type=MESH)

    loads = [pltpu.make_async_copy(a, b, load_sem.at[i]) for i, (a, b) in enumerate([
        (latent, latent_v), (w1, w1_v), (w2, w2_v), (w_in, w_in_v), (w_out, w_out_v), (cot, cot_v), (feat, feat_v),
        (anchor, anchor_v), (frac, frac_v)])]
    for load in loads:
        load.start()
    own_touch = pltpu.make_async_copy(touch.at[0], table_v.at[me], touch_own)
    own_touch.start()

    loads[0].wait()
    for c, y in enumerate((0, 1, 14, 15)):
        column = jnp.concatenate([latent_v[x, y : y + 1, :].astype(f32) for x in range(16)], axis=0)
        cols_v[c] = column.astype(bf16)
        for i in range(2):
            corner_v[i, c // 2, c % 2] = column[14 * i : 14 * i + 2].astype(bf16)

    pl.semaphore_wait(barrier, len(greeted))
    moves = [
        (latent_v.at[pl.ds(0, 2)], hx_v.at[1], (low_x, gy)),
        (latent_v.at[pl.ds(14, 2)], hx_v.at[0], (high_x, gy)),
        (cols_v.at[pl.ds(0, 2)], hy_v.at[1], (gx, low_y)),
        (cols_v.at[pl.ds(2, 2)], hy_v.at[0], (gx, high_y)),
    ]
    for i, near_x in enumerate((low_x, high_x)):
        for j, near_y in enumerate((low_y, high_y)):
            moves.append((corner_v.at[i, j], hc_v.at[1 - i, 1 - j], (near_x, near_y)))
    sides = [pltpu.make_async_remote_copy(src_ref=a, dst_ref=b, send_sem=side_send.at[m], recv_sem=side_recv.at[m],
                                          device_id=device, device_id_type=MESH) for m, (a, b, device) in enumerate(moves)]
    for copy in sides:
        copy.start()
    for device in along_y:
        pltpu.make_async_remote_copy(src_ref=touch.at[0], dst_ref=table_v.at[me], send_sem=touch_send.at[0], recv_sem=touch_recv.at[0],
                                     device_id=device, device_id_type=MESH).start()

    for load in loads[1:3]:
        load.wait()
    spread_weight(w1_v, band1)
    spread_weight(w2_v, band2)

    for copy in sides:
        copy.wait()
    own_touch.wait()
    line = table_v.at[pl.ds(0, n_gy - 1)]
    pltpu.make_async_copy(line, line, touch_recv.at[0]).wait()
    mine = table_v.at[pl.ds(gx * n_gy, n_gy)]
    for device in along_x:
        pltpu.make_async_remote_copy(src_ref=mine, dst_ref=mine, send_sem=touch_send.at[1], recv_sem=touch_recv.at[1],
                                     device_id=device, device_id_type=MESH).start()
    convolve_first(gx, gy, n_gx, n_gy, latent_v, cols_v, hx_v, hy_v, hc_v, band1, rows, edge, hid, hcol)
    plane = table_v.at[pl.ds(0, count - n_gy)]
    pltpu.make_async_copy(plane, plane, touch_recv.at[1]).wait()
    to_smem = pltpu.make_async_copy(table_v, table_s, smem_sem)
    to_smem.start()
    convolve_second(latent_v, band2, rows, hid, hcol, tiles)
    to_smem.wait()
    pltpu.make_async_copy(line, line, touch_send.at[0]).wait()
    pltpu.make_async_copy(plane, plane, touch_send.at[1]).wait()

    def pick(k, carry):
        wanted = table_s[lax.rem(me + k, count), 0, me]
        want_out[k] = wanted
        tile = tiles[jnp.maximum(wanted, 0)]
        outgoing[k] = jnp.where(wanted >= 0, tile, jnp.zeros_like(tile))
        return carry

    lax.fori_loop(0, count, pick, 0, unroll=8)
    part_slots = count // CHUNKS

    def wait_for(ref, sem):
        pltpu.make_async_copy(ref, ref, sem).wait()

    for g, (first, last) in enumerate(GROUPS):

        def send_tile(k, carry):
            pltpu.make_async_remote_copy(src_ref=outgoing.at[k], dst_ref=received.at[k], send_sem=tile_send, recv_sem=tile_recv.at[g],
                                         device_id=device_at(k), device_id_type=MESH).start()
            return carry

        lax.fori_loop(max(1, first), last, send_tile, 0)
    received[0] = outgoing[0]
    for load in loads[3:]:
        load.wait()
    wt[...] = w_in_v[...].T
    wide = w_out_v[...].astype(f32).T
    wo[...] = jnp.concatenate([wide, wide, wide, jnp.zeros_like(wide)], axis=1).astype(bf16)

    def weigh(i, carry):
        span = pl.ds(pl.multiple_of(i * PB, PB), PB)
        place = anchor_v[:, span]
        offset = frac_v[:, span]
        cell = lax.broadcasted_iota(jnp.int32, (16, PB), 0)
        off_x = (cell >> 2) - ((place >> 4) & 3)
        off_y = (cell & 3) - ((place >> 2) & 3)
        off_z = lax.broadcasted_iota(jnp.int32, (4, PB), 0) - (place & 3)
        dist_x = offset[0:1] - off_x.astype(f32)
        dist_y = offset[1:2] - off_y.astype(f32)
        dist_z = offset[2:3] - off_z.astype(f32)
        beside = jnp.logical_and(jnp.abs(off_x) <= 1, jnp.abs(off_y) <= 1)
        kxy = jnp.where(beside, jnp.exp(-(dist_x * dist_x + dist_y * dist_y)), 0.0)
        kz = jnp.where(jnp.abs(off_z) <= 1, jnp.exp(-(dist_z * dist_z)), 0.0)
        wxy = (kxy / jnp.sum(kxy, axis=0, keepdims=True)).astype(bf16)
        wz_v[:, span] = kz / jnp.sum(kz, axis=0, keepdims=True)
        distance = (me + count - (place >> 6)) & (count - 1)
        distance = jnp.broadcast_to(distance.astype(f32), (16, PB)).astype(bf16)
        zero = jnp.zeros_like(wxy)
        for k in range(count):
            near[k * 16 : (k + 1) * 16, span] = jnp.where(distance == bf16(k), wxy, zero)
        return carry

    lax.fori_loop(0, blocks, weigh, 0)

    def prepare(i, carry):
        span = pl.ds(pl.multiple_of(i * PB, PB), PB)
        state[:, span] = jnp.dot(wt[:, 64:], feat_v[:, span], preferred_element_type=f32)
        given = cot_v[:, span]
        high = given.astype(bf16).astype(f32)
        rest = given - high
        mid = rest.astype(bf16).astype(f32)
        pieces = jnp.concatenate([high, mid, rest - mid, jnp.zeros_like(high)], axis=0).astype(bf16)
        lift[:, span] = jnp.dot(wo[...], pieces, preferred_element_type=f32)
        return carry

    lax.fori_loop(0, blocks, prepare, 0)

    for g, (first, last) in enumerate(GROUPS):
        arrived = max(1, first)
        wait_for(received.at[pl.ds(arrived, last - arrived)], tile_recv.at[g])
        turned = received[first:last].reshape((last - first) * 16, 256).T
        for i in range(blocks):
            span = slice(i * PB, (i + 1) * PB)
            value = jnp.dot(turned, near[first * 16 : last * 16, span], preferred_element_type=f32)
            mixed[:, span] = value if g == 0 else mixed[:, span] + value

    for i in range(particles // SPAN):
        span = slice(i * SPAN, (i + 1) * SPAN)
        wz = wz_v[:, span]
        sampled = mixed[0:64, span] * wz[0:1]
        for z in range(1, 4):
            sampled = sampled + mixed[z * 64 : z * 64 + 64, span] * wz[z : z + 1]
        state[:, span] += jnp.dot(wt[:, :64], sampled.astype(bf16), preferred_element_type=f32)
        for top in range(0, 256, STRIP):
            strip = slice(top, top + STRIP)
            value, slope = gelu_pair(state[strip, span])
            active[strip, span] = value.astype(bf16)
            grad_pre[strip, span] = (lift[strip, span] * slope).astype(bf16)
        back = jnp.dot(w_in_v[0:64, :], grad_pre[:, span], preferred_element_type=f32)
        for z in range(4):
            spread[z * 64 : z * 64 + 64, span] = (back * wz[z : z + 1]).astype(bf16)

    def scatter(q, carry):
        band = pl.ds(pl.multiple_of(q * part_slots * 16, part_slots * 16), part_slots * 16)
        value = lax.dot_general(near[band, :], spread[...], (((1,), (1,)), ((), ())), preferred_element_type=f32)
        part[pl.ds(q * part_slots, part_slots)] = value.astype(bf16).reshape(part_slots, 16, 256)

        def send_back(j, inner):
            k = q * part_slots + j
            pltpu.make_async_remote_copy(src_ref=part.at[k], dst_ref=back_out.at[k], send_sem=back_send, recv_sem=back_recv,
                                         device_id=device_at(count - k), device_id_type=MESH).start()
            return inner

        return lax.fori_loop(jnp.where(q == 0, 1, 0), part_slots, send_back, carry)

    lax.fori_loop(0, CHUNKS, scatter, 0)
    own_back = pltpu.make_async_copy(part.at[0], back_out.at[0], back_own)
    own_back.start()

    def finish(i, carry):
        span = pl.ds(pl.multiple_of(i * PB, PB), PB)
        pred_v[:, span] = jnp.dot(w_out_v[...], active[:, span], preferred_element_type=f32)
        feat_v[:, span] = jnp.dot(w_in_v[64:, :], grad_pre[:, span], preferred_element_type=f32).astype(bf16)
        return carry

    lax.fori_loop(0, blocks, finish, 0)
    stores = [pltpu.make_async_copy(pred_v, pred_out, store_sem.at[0]), pltpu.make_async_copy(feat_v, grads_out, store_sem.at[1])]
    for store in stores:
        store.start()
    wait_for(outgoing.at[pl.ds(0, count - 1)], tile_send)
    sent = part.at[pl.ds(0, count - 1)]
    pltpu.make_async_copy(sent, sent, back_send).wait()
    own_back.wait()
    for store in stores:
        store.wait()
    landed = back_out.at[pl.ds(0, count - 1)]
    pltpu.make_async_copy(landed, landed, back_recv).wait()


def window(latent, touch, w1, w2, w_in, w_out, anchor, frac, feat, cot, n_gx, n_gy):
    hbm = pl.BlockSpec(memory_space=pltpu.HBM)
    smem = pl.BlockSpec(memory_space=pltpu.SMEM)
    bf, f32, i32 = jnp.bfloat16, jnp.float32, jnp.int32
    count = n_gx * n_gy
    particles = anchor.shape[1]
    dma = pltpu.SemaphoreType.DMA
    vmem = lambda a: pltpu.VMEM(a.shape, a.dtype)
    shaped = jax.ShapeDtypeStruct
    return pl.pallas_call(
        functools.partial(window_kernel, n_gx=n_gx, n_gy=n_gy),
        in_specs=[hbm] * 10,
        out_specs=[hbm, hbm, hbm, smem],
        out_shape=[shaped((4, particles), f32), shaped((256, particles), bf), shaped((count, 16, 256), bf), shaped((count,), i32)],
        scratch_shapes=[
            vmem(latent), pltpu.VMEM((4, 16, 1024), bf), pltpu.VMEM((2, 2, 2, 2, 1024), bf), vmem(w1), vmem(w2), vmem(w_in), vmem(w_out), vmem(anchor), vmem(frac), vmem(feat), vmem(cot),
            pltpu.VMEM((2, 2, 16, 1024), bf), pltpu.VMEM((2, 2, 16, 1024), bf), pltpu.VMEM((2, 2, 2, 2, 1024), bf),
            pltpu.VMEM((count, 1, count), i32), pltpu.SMEM((count, 1, count), i32),
            pltpu.VMEM((256, 3456), bf), pltpu.VMEM((256, 3456), bf), pltpu.VMEM((3, 20, 16, 1152), bf), pltpu.VMEM((9, 48, 1152), bf),
            pltpu.VMEM((18, 16, 1024), f32), pltpu.VMEM((2, 24, 1024), f32), pltpu.VMEM((64, 16, 256), bf),
            pltpu.VMEM((count, 16, 256), bf), pltpu.VMEM((count, 16, 256), bf),
            pltpu.VMEM((count * 16, particles), bf), pltpu.VMEM((256, particles), f32), pltpu.VMEM((256, particles), f32),
            pltpu.VMEM((256, particles), f32), pltpu.VMEM((4, particles), f32), pltpu.VMEM((256, 320), bf), pltpu.VMEM((256, 16), bf),
            pltpu.VMEM((256, particles), bf), pltpu.VMEM((256, particles), bf), pltpu.VMEM((256, particles), bf),
            pltpu.VMEM((count, 16, 256), bf), pltpu.VMEM((4, particles), f32),
            dma((9,)), dma((8,)), dma((8,)), dma(()), dma((2,)), dma((2,)), dma(()),
            dma(()), dma((len(GROUPS),)), dma(()), dma(()), dma(()), dma((2,)),
        ],
        compiler_params=pltpu.CompilerParams(collective_id=0, has_side_effects=True, vmem_limit_bytes=62 << 20),
        name="window",
    )(latent, touch, w1, w2, w_in, w_out, anchor, frac, feat, cot)


LANES = 4
PIECES = 4


def collect_kernel(want_ref, back, pred_in, grads_in, grid_out, pred_out, grads_out, back_v, pred_v, grads_v, grid_v, *rest):
    sums, load_sem, store_sem = rest[:LANES], rest[LANES], rest[LANES + 1]
    size = back_v.shape[0] // PIECES
    pieces = [pltpu.make_async_copy(back.at[pl.ds(i * size, size)], back_v.at[pl.ds(i * size, size)], load_sem.at[i]) for i in range(PIECES)]
    grads_load = pltpu.make_async_copy(grads_in, grads_v, load_sem.at[PIECES])
    pred_load = pltpu.make_async_copy(pred_in, pred_v, load_sem.at[PIECES + 1])
    for load in [grads_load, pred_load] + pieces:
        load.start()
    for sum_ref in sums:
        sum_ref[...] = jnp.zeros_like(sum_ref)

    def add(j, carry):
        for lane, sum_ref in enumerate(sums):
            k = j * LANES + lane
            wanted = want_ref[k]
            sum_ref[jnp.where(wanted >= 0, wanted, 64)] += back_v[k].astype(jnp.float32)
        return carry

    grads_load.wait()
    pred_load.wait()
    stores = [pltpu.make_async_copy(grads_v, grads_out, store_sem.at[4]), pltpu.make_async_copy(pred_v, pred_out, store_sem.at[5])]
    for store in stores:
        store.start()
    steps = size // LANES
    for i in range(PIECES):
        pieces[i].wait()
        lax.fori_loop(i * steps, (i + 1) * steps, add, 0, unroll=4)
    for tx in range(4):
        for ty in range(4):
            for tz in range(4):
                t = (tx * 4 + ty) * 4 + tz
                tile = sums[0][t]
                for sum_ref in sums[1:]:
                    tile = tile + sum_ref[t]
                for i in range(4):
                    grid_v[tx * 4 + i, ty * 4 : ty * 4 + 4, tz * 256 : tz * 256 + 256] = tile[i * 4 : i * 4 + 4]
        store = pltpu.make_async_copy(grid_v.at[pl.ds(tx * 4, 4)], grid_out.at[pl.ds(tx * 4, 4)], store_sem.at[tx])
        store.start()
        stores.append(store)
    for store in stores:
        store.wait()


def collect(want, back, predicted, grads):
    hbm = pl.BlockSpec(memory_space=pltpu.HBM)
    shaped = jax.ShapeDtypeStruct
    vmem = lambda a: pltpu.VMEM(a.shape, a.dtype)
    grid = shaped((16, 16, 1024), jnp.float32)
    return pl.pallas_call(
        collect_kernel,
        in_specs=[pl.BlockSpec(memory_space=pltpu.SMEM), hbm, hbm, hbm],
        out_specs=[hbm, hbm, hbm],
        out_shape=[grid, shaped(predicted.shape, predicted.dtype), shaped(grads.shape, grads.dtype)],
        scratch_shapes=[vmem(back), vmem(predicted), vmem(grads), vmem(grid)] + [pltpu.VMEM((65, 16, 256), jnp.float32)] * LANES
        + [pltpu.SemaphoreType.DMA((PIECES + 2,)), pltpu.SemaphoreType.DMA((6,))],
        compiler_params=pltpu.CompilerParams(vmem_limit_bytes=62 << 20),
        name="collect",
    )(want, back, predicted, grads)


def make_body(n_gx, n_gy):
    def body(latent, conv_first, conv_second, w_in, w_out, touch, anchor, frac, pfeat, cotangent):
        predicted, grads, back, want = window(
            latent, touch.reshape(1, 1, -1), conv_first, conv_second, w_in, w_out, anchor.reshape(1, -1), frac, pfeat, cotangent, n_gx, n_gy)
        grid_grad, predicted, grads = collect(want, back, predicted, grads)
        return (predicted, grads, grid_grad)

    return body


def solution(mesh):
    rows = P(("gx", "gy"), None)
    cols = P(None, ("gx", "gy"))
    grid = P("gx", "gy", None)
    return jax.shard_map(
        make_body(mesh.shape["gx"], mesh.shape["gy"]),
        mesh=mesh,
        in_specs=(grid, P(), P(), P(), P(), rows, P(("gx", "gy")), cols, cols, cols),
        out_specs=(cols, cols, grid),
        check_vma=False,
    )
```

```python
import functools

import jax
import jax.numpy as jnp
from jax import lax
from jax.experimental import pallas as pl
from jax.experimental.pallas import tpu as pltpu
from jax.sharding import PartitionSpec as P


def gelu_pair(x):
    k = 0.7978845608028654
    c = 0.044715 * k
    x2 = x * x
    share = 0.5 * jnp.tanh(x * (k + c * x2)) + 0.5
    slope = share * (1.0 + (1.0 - share) * (x * (2.0 * k + 6.0 * c * x2)))
    return x * share, slope


def gelu(x):
    return 0.5 * x * (1.0 + jnp.tanh(0.7978845608028654 * x * (1.0 + 0.044715 * (x * x))))


def pad_z(v):
    gap = jnp.zeros((v.shape[0], 64), v.dtype)
    return jnp.concatenate([gap, v, gap], axis=1)


def spread_weight(w_ref, band_ref):
    for k in range(9):
        tap = w_ref[:, k * 192 : (k + 1) * 192]
        for j in range(4):
            parts = [jnp.zeros((64, j * 64), tap.dtype)] * (j > 0) + [tap] + [jnp.zeros((64, 192 - j * 64), tap.dtype)] * (j < 3)
            band_ref[j * 64 : (j + 1) * 64, k * 384 : (k + 1) * 384] = jnp.concatenate(parts, axis=1)


def shift_rows(stack_ref, index, tile, low, high):
    stack_ref[0, index] = jnp.concatenate([low, tile[:15]], axis=0).astype(jnp.bfloat16)
    stack_ref[1, index] = tile.astype(jnp.bfloat16)
    stack_ref[2, index] = jnp.concatenate([tile[1:], high], axis=0).astype(jnp.bfloat16)


def convolve_first(gx, gy, n_gx, n_gy, latent_ref, cols_ref, hx_ref, hy_ref, hc_ref, band1_ref, rows_ref, edge_ref, hid_ref, hcol_ref):
    f32 = jnp.float32
    left, right = gx > 0, gx < n_gx - 1
    down, up = gy > 0, gy < n_gy - 1
    x_side, y_side = (left, right), (down, up)

    def halo_col(side, j):
        mid = hy_ref[side, j].astype(f32)
        low = jnp.where(left, hc_ref[0, side, j].astype(f32), 0.0)
        high = jnp.where(right, hc_ref[1, side, j].astype(f32), 0.0)
        return pad_z(jnp.where(y_side[side], jnp.concatenate([low, mid, high], axis=0), 0.0))

    def own_col(y, c):
        low = [hx_ref[0, i, y : y + 1, :].astype(f32) for i in range(2)]
        high = [hx_ref[1, i, y : y + 1, :].astype(f32) for i in range(2)]
        low = jnp.where(left, jnp.concatenate(low, axis=0), 0.0)
        high = jnp.where(right, jnp.concatenate(high, axis=0), 0.0)
        return pad_z(jnp.concatenate([low, cols_ref[c].astype(f32), high], axis=0))

    lower = [halo_col(0, 0), halo_col(0, 1), own_col(0, 0)]
    upper = [own_col(15, 3), halo_col(1, 0), halo_col(1, 1)]
    fill = jnp.zeros((6, 1152), f32)
    for dx in range(3):
        for dy in range(3):
            edge_ref[dx * 3 + dy] = jnp.concatenate(
                [lower[dy][dx : dx + 18], fill, upper[dy][dx : dx + 18], fill], axis=0).astype(jnp.bfloat16)
    for x in range(20):
        if x < 2:
            tile = jnp.where(left, hx_ref[0, x].astype(f32), 0.0)
        elif x < 18:
            tile = latent_ref[x - 2].astype(f32)
        else:
            tile = jnp.where(right, hx_ref[1, x - 18].astype(f32), 0.0)
        shift_rows(rows_ref, x, pad_z(tile), lower[1][x : x + 1], upper[1][x : x + 1])

    row24 = lax.broadcasted_iota(jnp.int32, (24, 1), 0)
    inside = jnp.logical_and(jnp.logical_or(row24 > 0, left), jnp.logical_or(row24 != 17, right))

    for b in range(4):
        lanes = slice(b * 256, b * 256 + 384)
        taps = []
        for dx in range(3):
            for dy in range(3):
                taps.append(jnp.concatenate([rows_ref[dy, dx : dx + 18, :, lanes].reshape(288, 384), edge_ref[dx * 3 + dy, :, lanes]], axis=0))
        acc = lax.dot_general(jnp.concatenate(taps, axis=1), band1_ref[...], (((1,), (1,)), ((), ())), preferred_element_type=f32)
        acc = gelu(acc)
        out = slice(b * 256, b * 256 + 256)
        hid_ref[0, :, out] = jnp.where(left, acc[:16], 0.0)
        hid_ref[1:17, :, out] = acc[16:272].reshape(16, 16, 256)
        hid_ref[17, :, out] = jnp.where(right, acc[272:288], 0.0)
        hcol_ref[0, :, out] = jnp.where(jnp.logical_and(inside, down), acc[288:312], 0.0)
        hcol_ref[1, :, out] = jnp.where(jnp.logical_and(inside, up), acc[312:336], 0.0)


def convolve_second(latent_ref, band2_ref, rows_ref, hid_ref, hcol_ref, tiles_ref):
    f32 = jnp.float32
    low, high = pad_z(hcol_ref[0]), pad_z(hcol_ref[1])
    for x in range(18):
        shift_rows(rows_ref, x, pad_z(hid_ref[x]), low[x : x + 1], high[x : x + 1])

    for b in range(4):
        lanes = slice(b * 256, b * 256 + 384)
        taps = [rows_ref[dy, dx : dx + 16, :, lanes].reshape(256, 384) for dx in range(3) for dy in range(3)]
        acc = lax.dot_general(jnp.concatenate(taps, axis=1), band2_ref[...], (((1,), (1,)), ((), ())), preferred_element_type=f32)
        acc = acc.reshape(16, 16, 256) + latent_ref[:, :, b * 256 : b * 256 + 256].astype(f32)
        for tx in range(4):
            for ty in range(4):
                tile = [acc[tx * 4 + i, ty * 4 : ty * 4 + 4] for i in range(4)]
                tiles_ref[(tx * 4 + ty) * 4 + b] = jnp.concatenate(tile, axis=0).astype(jnp.bfloat16)


MESH = pl.DeviceIdType.MESH
PB = 1024
CHUNKS = 4
SPAN = 2048
STRIP = 16
GROUPS = ((0, 32), (32, 64), (64, 96), (96, 128))


def window_kernel(latent, touch, w1, w2, w_in, w_out, anchor, frac, feat, cot,
                  pred_out, grads_out, back_out, want_out,
                  latent_v, cols_v, corner_v, w1_v, w2_v, w_in_v, w_out_v, anchor_v, frac_v, feat_v, cot_v,
                  hx_v, hy_v, hc_v, table_v, table_s,
                  band1, band2, rows, edge, hid, hcol, tiles, outgoing, received,
                  near, state, lift, mixed, wz_v, wt, wo, active, grad_pre, spread, part, pred_v,
                  load_sem, side_send, side_recv, touch_own, touch_send, touch_recv, smem_sem,
                  tile_send, tile_recv, back_own, back_send, back_recv, store_sem, *, n_gx, n_gy):
    f32, bf16 = jnp.float32, jnp.bfloat16
    count = n_gx * n_gy
    particles = anchor.shape[1]
    blocks = particles // PB
    gx, gy = lax.axis_index("gx"), lax.axis_index("gy")
    me = gx * n_gy + gy

    def device_at(k):
        index = lax.rem(me + k, count)
        return (index // n_gy, lax.rem(index, n_gy))

    along_y = [(gx, lax.rem(gy + j, n_gy)) for j in range(1, n_gy)]
    along_x = [(lax.rem(gx + i, n_gx), gy) for i in range(1, n_gx)]
    low_x, high_x = lax.rem(gx + n_gx - 1, n_gx), lax.rem(gx + 1, n_gx)
    low_y, high_y = lax.rem(gy + n_gy - 1, n_gy), lax.rem(gy + 1, n_gy)
    diagonal = [(near_x, near_y) for near_x in (low_x, high_x) for near_y in (low_y, high_y)]
    barrier = pltpu.get_barrier_semaphore()
    greeted = diagonal + along_x + along_y
    for device in greeted:
        pl.semaphore_signal(barrier, inc=1, device_id=device, device_id_type=MESH)

    loads = [pltpu.make_async_copy(a, b, load_sem.at[i]) for i, (a, b) in enumerate([
        (latent, latent_v), (w1, w1_v), (w2, w2_v), (w_in, w_in_v), (w_out, w_out_v), (cot, cot_v), (feat, feat_v),
        (anchor, anchor_v), (frac, frac_v)])]
    for load in loads:
        load.start()
    own_touch = pltpu.make_async_copy(touch.at[0], table_v.at[me], touch_own)
    own_touch.start()

    loads[0].wait()
    for c, y in enumerate((0, 1, 14, 15)):
        column = jnp.concatenate([latent_v[x, y : y + 1, :].astype(f32) for x in range(16)], axis=0)
        cols_v[c] = column.astype(bf16)
        for i in range(2):
            corner_v[i, c // 2, c % 2] = column[14 * i : 14 * i + 2].astype(bf16)

    pl.semaphore_wait(barrier, len(greeted))
    moves = [
        (latent_v.at[pl.ds(0, 2)], hx_v.at[1], (low_x, gy)),
        (latent_v.at[pl.ds(14, 2)], hx_v.at[0], (high_x, gy)),
        (cols_v.at[pl.ds(0, 2)], hy_v.at[1], (gx, low_y)),
        (cols_v.at[pl.ds(2, 2)], hy_v.at[0], (gx, high_y)),
    ]
    for i, near_x in enumerate((low_x, high_x)):
        for j, near_y in enumerate((low_y, high_y)):
            moves.append((corner_v.at[i, j], hc_v.at[1 - i, 1 - j], (near_x, near_y)))
    sides = [pltpu.make_async_remote_copy(src_ref=a, dst_ref=b, send_sem=side_send.at[m], recv_sem=side_recv.at[m],
                                          device_id=device, device_id_type=MESH) for m, (a, b, device) in enumerate(moves)]
    for copy in sides:
        copy.start()
    for device in along_y:
        pltpu.make_async_remote_copy(src_ref=touch.at[0], dst_ref=table_v.at[me], send_sem=touch_send.at[0], recv_sem=touch_recv.at[0],
                                     device_id=device, device_id_type=MESH).start()

    for load in loads[1:3]:
        load.wait()
    spread_weight(w1_v, band1)
    spread_weight(w2_v, band2)

    for copy in sides:
        copy.wait()
    own_touch.wait()
    line = table_v.at[pl.ds(0, n_gy - 1)]
    pltpu.make_async_copy(line, line, touch_recv.at[0]).wait()
    mine = table_v.at[pl.ds(gx * n_gy, n_gy)]
    for device in along_x:
        pltpu.make_async_remote_copy(src_ref=mine, dst_ref=mine, send_sem=touch_send.at[1], recv_sem=touch_recv.at[1],
                                     device_id=device, device_id_type=MESH).start()
    convolve_first(gx, gy, n_gx, n_gy, latent_v, cols_v, hx_v, hy_v, hc_v, band1, rows, edge, hid, hcol)
    plane = table_v.at[pl.ds(0, count - n_gy)]
    pltpu.make_async_copy(plane, plane, touch_recv.at[1]).wait()
    to_smem = pltpu.make_async_copy(table_v, table_s, smem_sem)
    to_smem.start()
    convolve_second(latent_v, band2, rows, hid, hcol, tiles)
    to_smem.wait()
    pltpu.make_async_copy(line, line, touch_send.at[0]).wait()
    pltpu.make_async_copy(plane, plane, touch_send.at[1]).wait()

    def pick(k, carry):
        wanted = table_s[lax.rem(me + k, count), 0, me]
        want_out[k] = wanted
        tile = tiles[jnp.maximum(wanted, 0)]
        outgoing[k] = jnp.where(wanted >= 0, tile, jnp.zeros_like(tile))
        return carry

    lax.fori_loop(0, count, pick, 0, unroll=8)
    part_slots = count // CHUNKS

    def wait_for(ref, sem):
        pltpu.make_async_copy(ref, ref, sem).wait()

    for g, (first, last) in enumerate(GROUPS):

        def send_tile(k, carry):
            pltpu.make_async_remote_copy(src_ref=outgoing.at[k], dst_ref=received.at[k], send_sem=tile_send, recv_sem=tile_recv.at[g],
                                         device_id=device_at(k), device_id_type=MESH).start()
            return carry

        lax.fori_loop(max(1, first), last, send_tile, 0)
    received[0] = outgoing[0]
    for load in loads[3:]:
        load.wait()
    wt[...] = w_in_v[...].T
    wide = w_out_v[...].astype(f32).T
    wo[...] = jnp.concatenate([wide, wide, wide, jnp.zeros_like(wide)], axis=1).astype(bf16)

    def weigh(i, carry):
        span = pl.ds(pl.multiple_of(i * PB, PB), PB)
        place = anchor_v[:, span]
        offset = frac_v[:, span]
        cell = lax.broadcasted_iota(jnp.int32, (16, PB), 0)
        off_x = (cell >> 2) - ((place >> 4) & 3)
        off_y = (cell & 3) - ((place >> 2) & 3)
        off_z = lax.broadcasted_iota(jnp.int32, (4, PB), 0) - (place & 3)
        dist_x = offset[0:1] - off_x.astype(f32)
        dist_y = offset[1:2] - off_y.astype(f32)
        dist_z = offset[2:3] - off_z.astype(f32)
        beside = jnp.logical_and(jnp.abs(off_x) <= 1, jnp.abs(off_y) <= 1)
        kxy = jnp.where(beside, jnp.exp(-(dist_x * dist_x + dist_y * dist_y)), 0.0)
        kz = jnp.where(jnp.abs(off_z) <= 1, jnp.exp(-(dist_z * dist_z)), 0.0)
        wxy = (kxy / jnp.sum(kxy, axis=0, keepdims=True)).astype(bf16)
        wz_v[:, span] = kz / jnp.sum(kz, axis=0, keepdims=True)
        distance = (me + count - (place >> 6)) & (count - 1)
        distance = jnp.broadcast_to(distance.astype(f32), (16, PB)).astype(bf16)
        zero = jnp.zeros_like(wxy)
        for k in range(count):
            near[k * 16 : (k + 1) * 16, span] = jnp.where(distance == bf16(k), wxy, zero)
        return carry

    lax.fori_loop(0, blocks, weigh, 0)

    def prepare(i, carry):
        span = pl.ds(pl.multiple_of(i * PB, PB), PB)
        state[:, span] = jnp.dot(wt[:, 64:], feat_v[:, span], preferred_element_type=f32)
        given = cot_v[:, span]
        high = given.astype(bf16).astype(f32)
        rest = given - high
        mid = rest.astype(bf16).astype(f32)
        pieces = jnp.concatenate([high, mid, rest - mid, jnp.zeros_like(high)], axis=0).astype(bf16)
        lift[:, span] = jnp.dot(wo[...], pieces, preferred_element_type=f32)
        return carry

    lax.fori_loop(0, blocks, prepare, 0)

    for g, (first, last) in enumerate(GROUPS):
        arrived = max(1, first)
        wait_for(received.at[pl.ds(arrived, last - arrived)], tile_recv.at[g])
        turned = received[first:last].reshape((last - first) * 16, 256).T
        for i in range(blocks):
            span = slice(i * PB, (i + 1) * PB)
            value = jnp.dot(turned, near[first * 16 : last * 16, span], preferred_element_type=f32)
            mixed[:, span] = value if g == 0 else mixed[:, span] + value

    for i in range(particles // SPAN):
        span = slice(i * SPAN, (i + 1) * SPAN)
        wz = wz_v[:, span]
        sampled = mixed[0:64, span] * wz[0:1]
        for z in range(1, 4):
            sampled = sampled + mixed[z * 64 : z * 64 + 64, span] * wz[z : z + 1]
        state[:, span] += jnp.dot(wt[:, :64], sampled.astype(bf16), preferred_element_type=f32)
        for top in range(0, 256, STRIP):
            strip = slice(top, top + STRIP)
            value, slope = gelu_pair(state[strip, span])
            active[strip, span] = value.astype(bf16)
            grad_pre[strip, span] = (lift[strip, span] * slope).astype(bf16)
        back = jnp.dot(w_in_v[0:64, :], grad_pre[:, span], preferred_element_type=f32)
        for z in range(4):
            spread[z * 64 : z * 64 + 64, span] = (back * wz[z : z + 1]).astype(bf16)

    def scatter(q, carry):
        band = pl.ds(pl.multiple_of(q * part_slots * 16, part_slots * 16), part_slots * 16)
        value = lax.dot_general(near[band, :], spread[...], (((1,), (1,)), ((), ())), preferred_element_type=f32)
        part[pl.ds(q * part_slots, part_slots)] = value.astype(bf16).reshape(part_slots, 16, 256)

        def send_back(j, inner):
            k = q * part_slots + j
            pltpu.make_async_remote_copy(src_ref=part.at[k], dst_ref=back_out.at[k], send_sem=back_send, recv_sem=back_recv,
                                         device_id=device_at(count - k), device_id_type=MESH).start()
            return inner

        return lax.fori_loop(jnp.where(q == 0, 1, 0), part_slots, send_back, carry)

    lax.fori_loop(0, CHUNKS, scatter, 0)
    own_back = pltpu.make_async_copy(part.at[0], back_out.at[0], back_own)
    own_back.start()

    def finish(i, carry):
        span = pl.ds(pl.multiple_of(i * PB, PB), PB)
        pred_v[:, span] = jnp.dot(w_out_v[...], active[:, span], preferred_element_type=f32)
        feat_v[:, span] = jnp.dot(w_in_v[64:, :], grad_pre[:, span], preferred_element_type=f32).astype(bf16)
        return carry

    lax.fori_loop(0, blocks, finish, 0)
    stores = [pltpu.make_async_copy(pred_v, pred_out, store_sem.at[0]), pltpu.make_async_copy(feat_v, grads_out, store_sem.at[1])]
    for store in stores:
        store.start()
    wait_for(outgoing.at[pl.ds(0, count - 1)], tile_send)
    sent = part.at[pl.ds(0, count - 1)]
    pltpu.make_async_copy(sent, sent, back_send).wait()
    own_back.wait()
    for store in stores:
        store.wait()
    landed = back_out.at[pl.ds(0, count - 1)]
    pltpu.make_async_copy(landed, landed, back_recv).wait()


def window(latent, touch, w1, w2, w_in, w_out, anchor, frac, feat, cot, n_gx, n_gy):
    hbm = pl.BlockSpec(memory_space=pltpu.HBM)
    smem = pl.BlockSpec(memory_space=pltpu.SMEM)
    bf, f32, i32 = jnp.bfloat16, jnp.float32, jnp.int32
    count = n_gx * n_gy
    particles = anchor.shape[1]
    dma = pltpu.SemaphoreType.DMA
    vmem = lambda a: pltpu.VMEM(a.shape, a.dtype)
    shaped = jax.ShapeDtypeStruct
    return pl.pallas_call(
        functools.partial(window_kernel, n_gx=n_gx, n_gy=n_gy),
        in_specs=[hbm] * 10,
        out_specs=[hbm, hbm, hbm, smem],
        out_shape=[shaped((4, particles), f32), shaped((256, particles), bf), shaped((count, 16, 256), bf), shaped((count,), i32)],
        scratch_shapes=[
            vmem(latent), pltpu.VMEM((4, 16, 1024), bf), pltpu.VMEM((2, 2, 2, 2, 1024), bf), vmem(w1), vmem(w2), vmem(w_in), vmem(w_out), vmem(anchor), vmem(frac), vmem(feat), vmem(cot),
            pltpu.VMEM((2, 2, 16, 1024), bf), pltpu.VMEM((2, 2, 16, 1024), bf), pltpu.VMEM((2, 2, 2, 2, 1024), bf),
            pltpu.VMEM((count, 1, count), i32), pltpu.SMEM((count, 1, count), i32),
            pltpu.VMEM((256, 3456), bf), pltpu.VMEM((256, 3456), bf), pltpu.VMEM((3, 20, 16, 1152), bf), pltpu.VMEM((9, 48, 1152), bf),
            pltpu.VMEM((18, 16, 1024), f32), pltpu.VMEM((2, 24, 1024), f32), pltpu.VMEM((64, 16, 256), bf),
            pltpu.VMEM((count, 16, 256), bf), pltpu.VMEM((count, 16, 256), bf),
            pltpu.VMEM((count * 16, particles), bf), pltpu.VMEM((256, particles), f32), pltpu.VMEM((256, particles), f32),
            pltpu.VMEM((256, particles), f32), pltpu.VMEM((4, particles), f32), pltpu.VMEM((256, 320), bf), pltpu.VMEM((256, 16), bf),
            pltpu.VMEM((256, particles), bf), pltpu.VMEM((256, particles), bf), pltpu.VMEM((256, particles), bf),
            pltpu.VMEM((count, 16, 256), bf), pltpu.VMEM((4, particles), f32),
            dma((9,)), dma((8,)), dma((8,)), dma(()), dma((2,)), dma((2,)), dma(()),
            dma(()), dma((len(GROUPS),)), dma(()), dma(()), dma(()), dma((2,)),
        ],
        compiler_params=pltpu.CompilerParams(collective_id=0, has_side_effects=True, vmem_limit_bytes=62 << 20),
        name="window",
    )(latent, touch, w1, w2, w_in, w_out, anchor, frac, feat, cot)


LANES = 4
PIECES = 4


def collect_kernel(want_ref, back, pred_in, grads_in, grid_out, pred_out, grads_out, back_v, pred_v, grads_v, grid_v, *rest):
    sums, load_sem, store_sem = rest[:LANES], rest[LANES], rest[LANES + 1]
    size = back_v.shape[0] // PIECES
    pieces = [pltpu.make_async_copy(back.at[pl.ds(i * size, size)], back_v.at[pl.ds(i * size, size)], load_sem.at[i]) for i in range(PIECES)]
    grads_load = pltpu.make_async_copy(grads_in, grads_v, load_sem.at[PIECES])
    pred_load = pltpu.make_async_copy(pred_in, pred_v, load_sem.at[PIECES + 1])
    for load in [grads_load, pred_load] + pieces:
        load.start()
    for sum_ref in sums:
        sum_ref[...] = jnp.zeros_like(sum_ref)

    def add(j, carry):
        for lane, sum_ref in enumerate(sums):
            k = j * LANES + lane
            wanted = want_ref[k]
            sum_ref[jnp.where(wanted >= 0, wanted, 64)] += back_v[k].astype(jnp.float32)
        return carry

    grads_load.wait()
    pred_load.wait()
    stores = [pltpu.make_async_copy(grads_v, grads_out, store_sem.at[4]), pltpu.make_async_copy(pred_v, pred_out, store_sem.at[5])]
    for store in stores:
        store.start()
    steps = size // LANES
    for i in range(PIECES):
        pieces[i].wait()
        lax.fori_loop(i * steps, (i + 1) * steps, add, 0, unroll=4)
    for tx in range(4):
        for ty in range(4):
            for tz in range(4):
                t = (tx * 4 + ty) * 4 + tz
                tile = sums[0][t]
                for sum_ref in sums[1:]:
                    tile = tile + sum_ref[t]
                for i in range(4):
                    grid_v[tx * 4 + i, ty * 4 : ty * 4 + 4, tz * 256 : tz * 256 + 256] = tile[i * 4 : i * 4 + 4]
        store = pltpu.make_async_copy(grid_v.at[pl.ds(tx * 4, 4)], grid_out.at[pl.ds(tx * 4, 4)], store_sem.at[tx])
        store.start()
        stores.append(store)
    for store in stores:
        store.wait()


def collect(want, back, predicted, grads):
    hbm = pl.BlockSpec(memory_space=pltpu.HBM)
    shaped = jax.ShapeDtypeStruct
    vmem = lambda a: pltpu.VMEM(a.shape, a.dtype)
    grid = shaped((16, 16, 1024), jnp.float32)
    return pl.pallas_call(
        collect_kernel,
        in_specs=[pl.BlockSpec(memory_space=pltpu.SMEM), hbm, hbm, hbm],
        out_specs=[hbm, hbm, hbm],
        out_shape=[grid, shaped(predicted.shape, predicted.dtype), shaped(grads.shape, grads.dtype)],
        scratch_shapes=[vmem(back), vmem(predicted), vmem(grads), vmem(grid)] + [pltpu.VMEM((65, 16, 256), jnp.float32)] * LANES
        + [pltpu.SemaphoreType.DMA((PIECES + 2,)), pltpu.SemaphoreType.DMA((6,))],
        compiler_params=pltpu.CompilerParams(vmem_limit_bytes=62 << 20),
        name="collect",
    )(want, back, predicted, grads)


def make_body(n_gx, n_gy):
    def body(latent, conv_first, conv_second, w_in, w_out, touch, anchor, frac, pfeat, cotangent):
        predicted, grads, back, want = window(
            latent, touch.reshape(1, 1, -1), conv_first, conv_second, w_in, w_out, anchor.reshape(1, -1), frac, pfeat, cotangent, n_gx, n_gy)
        grid_grad, predicted, grads = collect(want, back, predicted, grads)
        return (predicted, grads, grid_grad)

    return body


def solution(mesh):
    rows = P(("gx", "gy"), None)
    cols = P(None, ("gx", "gy"))
    grid = P("gx", "gy", None)
    return jax.shard_map(
        make_body(mesh.shape["gx"], mesh.shape["gy"]),
        mesh=mesh,
        in_specs=(grid, P(), P(), P(), P(), rows, P(("gx", "gy")), cols, cols, cols),
        out_specs=(cols, cols, grid),
        check_vma=False,
    )
```
